512 devices in a mesh: mode: 64 (over x, y, core), rank: 8 (over z).
Axes of the slice: x: 4, y: 8, z: 8, core: 2. Of those that a mesh axis runs over, the one named last changes fastest.
Arguments:
- start_core: float32 [1024, 128, 128], P('mode', 'rank'), may hold values from -108 to 108
- right_side: float32 [1024, 128, 128], P('mode', 'rank'), may hold values from -108 to 108
- left_interface: float32 [3, 128, 128], replicated, may hold values from -1 to 2
- right_interface: float32 [3, 128, 128], replicated, may hold values from -1 to 2
- couplings: float32 [3, 3, 3, 1024], P(None, None, None, 'mode'), may hold values from -5 to 5
Outputs:
- orthonormal_core: float32 [1024, 128, 128], P('mode', 'rank')
- triangle: float32 [128, 128], replicated
- next_interface: float32 [3, 128, 128], P(None, 'rank')
The draws below stay inside these ranges and needn't reach their ends.
All inputs are finite; a program needn't handle non-finite values.
Results may differ from the reference program's by a relative error of at most 0.00027.
Values sent between devices are 32-bit elements; how exact they have to be, the bound alone decides.
No kernel may reach another device: no remote copies, remote signals or barrier semaphores. Data moves between devices by JAX's collectives and lax.ppermute only.
A program may use at most 64 MiB of HBM per device.

```python
import math
import jax
import jax.numpy as jnp
from jax import lax

R = 128
OPR = 3
MODE = 1024


def draw_field(key):
    first, second = jax.random.split(key)
    ramp = 1.0 + 2.0 * jnp.arange(MODE, dtype=jnp.float32) / max(MODE - 1, 1)
    scales = jnp.exp(jax.random.uniform(second, (R,), minval=math.log(0.3), maxval=math.log(3.0)))
    values = jax.random.truncated_normal(first, -4.0, 4.0, (MODE, R, R))
    return (values * ramp[:, None, None] * scales[None, None, :]).astype(jnp.float32)


def draw_start_core(key, part):
    return draw_field(jax.random.fold_in(key, 11))


def draw_right_side(key, part):
    return draw_field(jax.random.fold_in(key, 23))


def draw_interface(key):
    values = jax.random.truncated_normal(key, -4.0, 4.0, (OPR, R, R)) / math.sqrt(R)
    first_slice = (jnp.arange(OPR) == 0)[:, None, None]
    identity = jnp.eye(R, dtype=jnp.float32)[None, :, :]
    return jnp.where(first_slice, 0.5 * values + identity, values).astype(jnp.float32)


def draw_left_interface(key, part):
    return draw_interface(jax.random.fold_in(key, 37))


def draw_right_interface(key, part):
    return draw_interface(jax.random.fold_in(key, 41))


def draw_couplings(key, part):
    first, second = jax.random.split(jax.random.fold_in(key, 53))
    raw = jax.random.truncated_normal(first, -4.0, 4.0, (OPR, OPR, 3, MODE))
    base = 0.2 * raw
    centre = jax.random.uniform(second, (MODE,), minval=1.0, maxval=2.0)
    outer = jnp.arange(OPR)[:, None, None, None]
    inner = jnp.arange(OPR)[None, :, None, None]
    offset = jnp.arange(3)[None, None, :, None]
    leading = (outer == 0) & (inner == 0)
    chosen = leading & (offset == 1)
    sides = leading & (offset != 1)
    values = jnp.where(sides, 1.2 * raw, base)
    return jnp.where(chosen, centre[None, None, None, :], values).astype(jnp.float32)


def setup_inputs(seed: int = 0) -> dict:
    key_list = jax.random.split(jax.random.key(seed), 6)
    start_core = draw_start_core(jax.random.fold_in(key_list[5], 71), 0)
    right_side = draw_right_side(jax.random.fold_in(key_list[5], 71), 0)
    left_interface = draw_left_interface(jax.random.fold_in(key_list[5], 71), 0)
    right_interface = draw_right_interface(jax.random.fold_in(key_list[5], 71), 0)
    couplings = draw_couplings(jax.random.fold_in(key_list[5], 71), 0)
    return dict(start_core=start_core, right_side=right_side, left_interface=left_interface, right_interface=right_interface, couplings=couplings)


highest = lax.Precision.HIGHEST

def banded(field, couplings, form):
    length = field.shape[1]
    padded = jnp.pad(field, ((0, 0), (1, 1), (0, 0), (0, 0)))
    total = jnp.einsum(form, couplings[:, :, 0, :], padded[:, 0:length], precision=highest)
    for offset in range(1, 3):
        total = total + jnp.einsum(form, couplings[:, :, offset, :], padded[:, offset:offset + length], precision=highest)
    return total

def apply_operator(field, left_interface, right_interface, couplings):
    contracted = jnp.einsum('ybc,icd->yibd', right_interface, field, precision=highest)
    coupled = banded(contracted, couplings, 'xyi,yibd->xibd')
    return jnp.einsum('xad,xibd->iba', left_interface, coupled, precision=highest)

def reference(start_core, right_side, left_interface, right_interface, couplings):
    scale = 1.0 / (R * MODE)
    applied = apply_operator(start_core, left_interface, right_interface, couplings)
    residual = right_side - applied
    image = apply_operator(residual, left_interface, right_interface, couplings)
    alpha = jnp.sum(residual * image) / jnp.sum(image * image)
    core = start_core + alpha * residual
    gram = jnp.einsum('ica,ida->cd', core, core, precision=highest) * scale
    lower = jnp.linalg.cholesky(gram)
    inverse = jax.scipy.linalg.solve_triangular(lower, jnp.eye(R, dtype=jnp.float32), lower=True)
    basis = jnp.einsum('bc,ica->iba', inverse, core, precision=highest)
    mixed = jnp.einsum('xad,ibd->xiba', left_interface, basis, precision=highest)
    moved = banded(mixed, couplings, 'xyi,xiba->yiba')
    interface = jnp.einsum('ipa,yiqa->yqp', basis, moved, precision=highest) * scale
    return (basis, lower.T, interface)
```

```python
import jax
import jax.numpy as jnp
from jax import lax
from jax.sharding import PartitionSpec as P

highest = lax.Precision.HIGHEST


def exchange(blocks, axis):
    return lax.all_to_all(blocks, axis, 0, 0, tiled=True)


def shards(start_core, right_side, left_interface, right_interface, couplings):
    height, piece, width = start_core.shape
    ranks = lax.axis_size("rank")
    slabs = lax.axis_size("mode")
    count = slabs * ranks
    own = height // ranks
    rank_index = lax.axis_index("rank")
    scale = 1.0 / (height * slabs * width)
    rows = 4 * width // slabs

    start = start_core.reshape(ranks, own, piece, width)
    right = right_side.reshape(ranks, own, piece, width)
    packed = jnp.concatenate([right[:, :1], start, right[:, 1:]], axis=1)
    mine = exchange(packed, "rank").transpose(1, 0, 2, 3).reshape(own + 2, width, width)

    table = lax.dynamic_slice_in_dim(couplings.reshape(27, height), rank_index * own, own, 1)
    forward = [(i, i + 1) for i in range(count - 1)]
    backward = [(target, source) for source, target in forward]

    def parcel(part, column):
        spread = jnp.broadcast_to(jnp.pad(column, ((0, 5), (0, 0))), (32, width))
        return jnp.concatenate([part.reshape(3 * width, width), spread], axis=0)

    low = lax.ppermute(parcel(mine[1:4], table[:, 1:2]), ("mode", "rank"), forward)
    high = lax.ppermute(parcel(mine[0:3], table[:, 0:1]), ("mode", "rank"), backward)
    low_field = low[: 3 * width].reshape(3, width, width)
    high_field = high[: 3 * width].reshape(3, width, width)
    field = jnp.concatenate([low_field[0:2], mine[1:3], high_field[1:3]])
    source = jnp.concatenate([low_field[2:3], mine[0:1], mine[3:4], high_field[0:1]])
    coupling = jnp.concatenate(
        [low[3 * width : 3 * width + 27, :1], table, high[3 * width : 3 * width + 27, :1]], axis=1
    ).reshape(3, 3, 3, 4)

    def banded(terms, weights, form):
        length = weights.shape[3]
        total = 0.0
        for offset in range(3):
            total = total + jnp.einsum(
                form, weights[:, :, offset], terms[:, offset : offset + length], precision=highest
            )
        return total

    def apply_operator(values, weights):
        contracted = jnp.einsum("ybc,icd->yibd", right_interface, values, precision=highest)
        coupled = banded(contracted, weights, "xyi,yibd->xibd")
        return jnp.einsum("xad,xibd->iba", left_interface, coupled, precision=highest)

    residual = source - apply_operator(field, coupling)
    inner = coupling[:, :, :, 1:3]
    image = apply_operator(residual, inner)
    owned = residual[1:3]
    along = jnp.sum(owned * image)
    energy = jnp.sum(image * image)

    pair = jnp.stack([field[1:5], residual])
    mixed = jnp.einsum("xad,uibd->uxiba", left_interface, pair, precision=highest)
    moved = jnp.stack([banded(mixed[u], inner, "xyi,xiba->yiba") for u in range(2)])
    both = pair[:, 1:3]
    products = jnp.einsum("uyiqa,wipa->uwyqp", moved, both, precision=highest)
    grams = jnp.einsum("uiqa,wipa->uwqp", both, both, precision=highest)[:, :, None]
    tables = jnp.concatenate([grams, products], axis=2)
    terms = [tables[0, 0], tables[0, 1] + tables[1, 0], tables[1, 1]]
    terms = [term.reshape(slabs, rows, width) for term in terms]
    sums = jnp.stack([along, energy])[:, None]
    tail = jnp.broadcast_to(jnp.pad(sums, ((0, 6), (0, 0))), (slabs, 8, width))
    blocks = jnp.concatenate(terms + [tail], axis=1)

    block = jnp.sum(exchange(blocks, "mode"), axis=0)
    block = jnp.sum(exchange(jnp.broadcast_to(block, (ranks,) + block.shape), "rank"), axis=0)
    alpha = block[3 * rows, 0] / block[3 * rows + 1, 0]
    block = block[:rows] + alpha * (block[rows : 2 * rows] + alpha * block[2 * rows : 3 * rows])
    whole = exchange(jnp.broadcast_to(block * scale, (slabs, rows, width)), "mode")
    whole = whole.reshape(4, width, width)

    lower = jnp.linalg.cholesky(whole[0])
    inverse = jax.scipy.linalg.solve_triangular(
        lower, jnp.eye(width, dtype=jnp.float32), lower=True
    )
    core = field[2:4] + alpha * owned
    basis = jnp.einsum("bc,ica->bia", inverse, core, precision=highest)
    basis = basis.reshape(ranks, piece, own, width).transpose(0, 2, 1, 3)
    output = exchange(basis, "rank").reshape(height, piece, width)
    inverse_rows = lax.dynamic_slice_in_dim(inverse, rank_index * piece, piece, 0)
    interface = jnp.einsum("qc,ycd->yqd", inverse_rows, whole[1:], precision=highest)
    interface = jnp.einsum("yqd,pd->yqp", interface, inverse, precision=highest)
    return (output, lower.T, interface)


def solution(mesh):
    placed = (
        P("mode", "rank", None),
        P("mode", "rank", None),
        P(),
        P(),
        P(None, None, None, "mode"),
    )
    return jax.shard_map(
        shards,
        mesh=mesh,
        in_specs=placed,
        out_specs=(P("mode", "rank", None), P(), P(None, "rank", None)),
        check_vma=False,
    )
```

```python
import jax
import jax.numpy as jnp
from jax import lax
from jax.experimental import pallas as pl
from jax.experimental.pallas import tpu as pltpu
from jax.sharding import PartitionSpec as P

highest = lax.Precision.HIGHEST
W = 128
HALF = W // 2


def exchange(blocks, axis):
    return lax.all_to_all(blocks, axis, 0, 0, tiled=True)


def product(left, right):
    return jnp.dot(left, right, precision=highest, preferred_element_type=jnp.float32)


def product_t(left, right):
    return lax.dot_general(
        left,
        right,
        (((1,), (1,)), ((), ())),
        precision=highest,
        preferred_element_type=jnp.float32,
    )


def iotas(shape):
    return lax.broadcasted_iota(jnp.int32, shape, 0), lax.broadcasted_iota(jnp.int32, shape, 1)


def local_kernel(
    mine, low, high, table, left_ref, right_ref, blocks, owned, terms, mixed, coupled, moved, pair
):
    def slot(index):
        return mine[:, index].reshape(W, W)

    fields = [low[0:W], low[W : 2 * W], slot(0), slot(1), high[0:W], high[W : 2 * W]]
    sources = [low[2 * W : 3 * W], slot(2), slot(3), high[2 * W : 3 * W]]
    weights = [(low, 3 * W), (table, 0), (table, 32), (high, 3 * W)]
    right_rows = right_ref[...].reshape(3 * W, W)
    left_rows = left_ref[...].reshape(3 * W, W)
    left_lanes = jnp.concatenate([left_ref[0], left_ref[1], left_ref[2]], axis=1)

    def contract(values):
        for k in range(0, len(values), 2):
            both = product(right_rows, jnp.concatenate(values[k : k + 2], axis=1))
            terms[k] = both[:, :W]
            terms[k + 1] = both[:, W:]

    def rows_of(place):
        ref, base = place
        return [jnp.broadcast_to(ref[base + t : base + t + 1, :], (8, W)) for t in range(27)]

    def couple(place, first):
        cs = rows_of(place)

        def step(chunk, carry):
            at = pl.multiple_of(chunk * 8, 8)
            sums = [None] * 3
            for offset in range(3):
                for beta in range(3):
                    value = terms[first + offset, pl.ds(beta * W + at, 8), :]
                    for alpha in range(3):
                        part = cs[alpha * 9 + beta * 3 + offset] * value
                        sums[alpha] = part if sums[alpha] is None else sums[alpha] + part
            for alpha in range(3):
                coupled[pl.ds(at, 8), alpha * W : (alpha + 1) * W] = sums[alpha]
            return carry

        lax.fori_loop(0, W // 8, step, 0, unroll=2)
        return product_t(coupled[...], left_lanes)

    contract(fields)
    residual = [sources[i] - couple(weights[i], i) for i in range(4)]
    for i in range(4):
        pair[i] = fields[i + 1]
        pair[4 + i] = residual[i]
    owned[0:W] = residual[1]
    owned[W : 2 * W] = residual[2]
    contract(residual)
    along = jnp.zeros((1, 1), jnp.float32)
    energy = jnp.zeros((1, 1), jnp.float32)
    for i in range(2):
        image = couple(weights[1 + i], i)
        along = along + jnp.sum(pair[5 + i] * image, keepdims=True)
        energy = energy + jnp.sum(image * image, keepdims=True)

    for u in range(2):
        stack = pair[4 * u : 4 * u + 4].reshape(4 * W, W)
        mixed[4 * u : 4 * u + 4] = product_t(stack, left_rows).reshape(4, W, 3 * W)
    for i in range(2):
        cs = rows_of(weights[1 + i])

        def step(chunk, carry):
            u = chunk // (W // 8)
            at = pl.multiple_of((chunk % (W // 8)) * 8, 8)
            sums = [None] * 3
            for offset in range(3):
                for alpha in range(3):
                    value = mixed[4 * u + i + offset, pl.ds(at, 8), alpha * W : (alpha + 1) * W]
                    for beta in range(3):
                        part = cs[alpha * 9 + beta * 3 + offset] * value
                        sums[beta] = part if sums[beta] is None else sums[beta] + part
            for beta in range(3):
                moved[u, pl.ds(beta * W + at, 8), i * W : (i + 1) * W] = sums[beta]
            return carry

        lax.fori_loop(0, 2 * (W // 8), step, 0, unroll=2)

    both = jnp.concatenate(
        [
            jnp.concatenate([pair[1], pair[2]], axis=1),
            jnp.concatenate([pair[5], pair[6]], axis=1),
        ],
        axis=0,
    )
    forms = [product_t(moved[u], both) for u in range(2)]
    tables = [forms[0][:, :W], forms[0][:, W:] + forms[1][:, :W], forms[1][:, W:]]
    square = product_t(both, both)
    grams = [square[:W, :W], square[:W, W:] + square[W:, :W], square[W:, W:]]
    row, lane = iotas((HALF, W))
    for version in range(3):
        gram = grams[version]
        upper, under = gram[:HALF], gram[HALF:]
        for part in range(6):
            blocks[pl.ds(8 * version + part, HALF, stride=24), :] = tables[version][
                part * HALF : (part + 1) * HALF
            ]
        fold = jnp.where(lane <= row + HALF, under, pltpu.roll(upper, HALF, 1))
        blocks[pl.ds(8 * version + 6, HALF, stride=24), :] = fold
        diagonal = jnp.sum(jnp.where(lane == row, upper, 0.0), axis=1, keepdims=True)
        extra = jnp.where(lane == 0, diagonal, 0.0)
        if version == 0:
            extra = jnp.where(lane == 1, along, jnp.where(lane == 2, energy, extra))
        blocks[pl.ds(8 * version + 7, HALF, stride=24), :] = extra


def local_part(mine, low, high, table, left_interface, right_interface):
    vmem = pl.BlockSpec(memory_space=pltpu.VMEM)
    return pl.pallas_call(
        local_kernel,
        out_shape=(
            jax.ShapeDtypeStruct((HALF * 24, W), jnp.float32),
            jax.ShapeDtypeStruct((2 * W, W), jnp.float32),
        ),
        in_specs=[vmem] * 6,
        out_specs=(vmem, vmem),
        scratch_shapes=[
            pltpu.VMEM((6, 3 * W, W), jnp.float32),
            pltpu.VMEM((8, W, 3 * W), jnp.float32),
            pltpu.VMEM((W, 3 * W), jnp.float32),
            pltpu.VMEM((2, 3 * W, 2 * W), jnp.float32),
            pltpu.VMEM((8, W, W), jnp.float32),
        ],
        name="local_part",
    )(mine, low, high, table, left_interface, right_interface)


def combine_kernel(got, out, alpha_ref, *, ranks, scale):
    parts = []
    for version in range(3):
        total = got[8 * version : 8 * version + 8]
        for source in range(1, ranks):
            total = total + got[24 * source + 8 * version : 24 * source + 8 * version + 8]
        parts.append(total)
    row, lane = iotas((8, W))
    along = jnp.sum(jnp.where((row == 7) & (lane == 1), parts[0], 0.0), keepdims=True)
    energy = jnp.sum(jnp.where((row == 7) & (lane == 2), parts[0], 0.0), keepdims=True)
    alpha = jnp.broadcast_to(along, (8, W)) / jnp.broadcast_to(energy, (8, W))
    alpha_ref[...] = alpha
    block = (parts[0] + alpha * (parts[1] + alpha * parts[2])) * scale
    for m in range(HALF):
        out[8 * m : 8 * m + 8] = block


def combine_part(got, ranks, scale):
    vmem = pl.BlockSpec(memory_space=pltpu.VMEM)

    def kernel(*refs):
        combine_kernel(*refs, ranks=ranks, scale=scale)

    return pl.pallas_call(
        kernel,
        out_shape=(
            jax.ShapeDtypeStruct((HALF * 8, W), jnp.float32),
            jax.ShapeDtypeStruct((8, W), jnp.float32),
        ),
        in_specs=[vmem],
        out_specs=(vmem, vmem),
        name="combine_part",
    )(got)


def unfold(whole):
    table = jnp.concatenate([whole[:, part] for part in range(6)]).reshape(3, W, W)
    fold, extra = whole[:, 6], whole[:, 7]
    row, lane = iotas((HALF, W))
    under = jnp.where(lane <= row + HALF, fold, 0.0)
    upper = jnp.where((lane > row) & (lane < HALF), jnp.roll(fold, HALF, 1), 0.0)
    upper = upper + jnp.where(lane == row, extra[:, :1], 0.0)
    half = jnp.concatenate([jnp.zeros((HALF, W)), under]) + jnp.pad(upper, ((0, HALF), (0, 0))).T
    row, lane = iotas((W, W))
    return jnp.where(lane <= row, half, half.T), table


def shards(start_core, right_side, left_interface, right_interface, couplings):
    height, piece, width = start_core.shape
    ranks = lax.axis_size("rank")
    slabs = lax.axis_size("mode")
    count = slabs * ranks
    own = height // ranks
    assert width == W and own == 2 and slabs == HALF
    rank_index = lax.axis_index("rank")
    scale = 1.0 / (height * slabs * width)

    start = start_core.reshape(ranks, own, piece, width)
    right = right_side.reshape(ranks, own, piece, width)
    mine = exchange(jnp.concatenate([start, right], axis=1), "rank")

    table = lax.dynamic_slice_in_dim(couplings.reshape(27, height), rank_index * own, own, 1)
    table = jnp.pad(table, ((0, 5), (0, 0))).T[:, :, None]
    table = jnp.broadcast_to(table, (own, 32, width)).reshape(own * 32, width)
    forward = [(i, i + 1) for i in range(count - 1)]
    backward = [(target, source) for source, target in forward]

    def parcel(source, column):
        parts = [mine[:, slot].reshape(width, width) for slot in (0, 1, source)]
        return jnp.concatenate(parts + [table[32 * column : 32 * column + 32]], axis=0)

    low = lax.ppermute(parcel(3, 1), ("mode", "rank"), forward)
    high = lax.ppermute(parcel(2, 0), ("mode", "rank"), backward)
    blocks, owned = local_part(mine, low, high, table, left_interface, right_interface)

    block = jnp.sum(exchange(blocks.reshape(slabs, 24, width), "mode"), axis=0)
    block = exchange(jnp.broadcast_to(block, (ranks, 24, width)), "rank")
    block, alpha = combine_part(block.reshape(ranks * 24, width), ranks, scale)
    whole = exchange(block.reshape(slabs, 8, width), "mode")

    gram, tables = unfold(whole)
    lower = jnp.linalg.cholesky(gram)
    inverse = jax.scipy.linalg.solve_triangular(
        lower, jnp.eye(width, dtype=jnp.float32), lower=True
    )
    field = mine[:, :2].transpose(1, 0, 2, 3).reshape(own, width, width)
    core = field + alpha[0, 0] * owned.reshape(own, width, width)
    basis = jnp.einsum("bc,ica->bia", inverse, core, precision=highest)
    basis = basis.reshape(ranks, piece, own, width).transpose(0, 2, 1, 3)
    output = exchange(basis, "rank").reshape(height, piece, width)
    inverse_rows = lax.dynamic_slice_in_dim(inverse, rank_index * piece, piece, 0)
    interface = jnp.einsum("qc,ycd->yqd", inverse_rows, tables, precision=highest)
    interface = jnp.einsum("yqd,pd->yqp", interface, inverse, precision=highest)
    return (output, lower.T, interface)


def solution(mesh):
    placed = (
        P("mode", "rank", None),
        P("mode", "rank", None),
        P(),
        P(),
        P(None, None, None, "mode"),
    )
    return jax.shard_map(
        shards,
        mesh=mesh,
        in_specs=placed,
        out_specs=(P("mode", "rank", None), P(), P(None, "rank", None)),
        check_vma=False,
    )
```

```python
import jax
import jax.numpy as jnp
from jax import lax
from jax.experimental import pallas as pl
from jax.experimental.pallas import tpu as pltpu
from jax.sharding import Mesh
from jax.sharding import PartitionSpec as P

highest = lax.Precision.HIGHEST
W = 128
HALF = W // 2
SIZE = 16


def exchange(blocks, axis):
    return lax.all_to_all(blocks, axis, 0, 0, tiled=True)


def product(left, right):
    return jnp.dot(left, right, precision=highest, preferred_element_type=jnp.float32)


def product_t(left, right):
    return lax.dot_general(
        left,
        right,
        (((1,), (1,)), ((), ())),
        precision=highest,
        preferred_element_type=jnp.float32,
    )


def iotas(shape):
    return lax.broadcasted_iota(jnp.int32, shape, 0), lax.broadcasted_iota(jnp.int32, shape, 1)


def local_kernel(
    mine, low, high, table, left_ref, right_ref, blocks, owned, terms, mixed, coupled, moved, pair
):
    def slot(index):
        return mine[:, index].reshape(W, W)

    fields = [low[0:W], low[W : 2 * W], slot(0), slot(1), high[0:W], high[W : 2 * W]]
    sources = [low[2 * W : 3 * W], slot(2), slot(3), high[2 * W : 3 * W]]
    weights = [(low, 3 * W), (table, 0), (table, 32), (high, 3 * W)]
    right_rows = right_ref[...].reshape(3 * W, W)
    left_rows = left_ref[...].reshape(3 * W, W)
    left_lanes = jnp.concatenate([left_ref[0], left_ref[1], left_ref[2]], axis=1)

    def contract(values):
        for k in range(0, len(values), 2):
            both = product(right_rows, jnp.concatenate(values[k : k + 2], axis=1))
            terms[k] = both[:, :W]
            terms[k + 1] = both[:, W:]

    def rows_of(place):
        ref, base = place
        return [jnp.broadcast_to(ref[base + t : base + t + 1, :], (8, W)) for t in range(27)]

    def couple(place, first):
        cs = rows_of(place)

        def step(chunk, carry):
            at = pl.multiple_of(chunk * 8, 8)
            sums = [None] * 3
            for offset in range(3):
                for beta in range(3):
                    value = terms[first + offset, pl.ds(beta * W + at, 8), :]
                    for alpha in range(3):
                        part = cs[alpha * 9 + beta * 3 + offset] * value
                        sums[alpha] = part if sums[alpha] is None else sums[alpha] + part
            for alpha in range(3):
                coupled[pl.ds(at, 8), alpha * W : (alpha + 1) * W] = sums[alpha]
            return carry

        lax.fori_loop(0, W // 8, step, 0, unroll=2)
        return product_t(coupled[...], left_lanes)

    contract(fields)
    residual = [sources[i] - couple(weights[i], i) for i in range(4)]
    for i in range(4):
        pair[i] = fields[i + 1]
        pair[4 + i] = residual[i]
    owned[0:W] = residual[1]
    owned[W : 2 * W] = residual[2]
    contract(residual)
    along = jnp.zeros((1, 1), jnp.float32)
    energy = jnp.zeros((1, 1), jnp.float32)
    for i in range(2):
        image = couple(weights[1 + i], i)
        along = along + jnp.sum(pair[5 + i] * image, keepdims=True)
        energy = energy + jnp.sum(image * image, keepdims=True)

    for u in range(2):
        stack = pair[4 * u : 4 * u + 4].reshape(4 * W, W)
        mixed[4 * u : 4 * u + 4] = product_t(stack, left_rows).reshape(4, W, 3 * W)
    for i in range(2):
        cs = rows_of(weights[1 + i])

        def step(chunk, carry):
            u = chunk // (W // 8)
            at = pl.multiple_of((chunk % (W // 8)) * 8, 8)
            sums = [None] * 3
            for offset in range(3):
                for alpha in range(3):
                    value = mixed[4 * u + i + offset, pl.ds(at, 8), alpha * W : (alpha + 1) * W]
                    for beta in range(3):
                        part = cs[alpha * 9 + beta * 3 + offset] * value
                        sums[beta] = part if sums[beta] is None else sums[beta] + part
            for beta in range(3):
                moved[u, pl.ds(beta * W + at, 8), i * W : (i + 1) * W] = sums[beta]
            return carry

        lax.fori_loop(0, 2 * (W // 8), step, 0, unroll=2)

    both = jnp.concatenate(
        [
            jnp.concatenate([pair[1], pair[2]], axis=1),
            jnp.concatenate([pair[5], pair[6]], axis=1),
        ],
        axis=0,
    )
    forms = [product_t(moved[u], both) for u in range(2)]
    tables = [forms[0][:, :W], forms[0][:, W:] + forms[1][:, :W], forms[1][:, W:]]
    square = product_t(both, both)
    grams = [square[:W, :W], square[:W, W:] + square[W:, :W], square[W:, W:]]
    row, lane = iotas((HALF, W))
    for version in range(3):
        gram = grams[version]
        upper, under = gram[:HALF], gram[HALF:]
        for part in range(6):
            blocks[pl.ds(8 * version + part, HALF, stride=24), :] = tables[version][
                part * HALF : (part + 1) * HALF
            ]
        fold = jnp.where(lane <= row + HALF, under, pltpu.roll(upper, HALF, 1))
        blocks[pl.ds(8 * version + 6, HALF, stride=24), :] = fold
        diagonal = jnp.sum(jnp.where(lane == row, upper, 0.0), axis=1, keepdims=True)
        extra = jnp.where(lane == 0, diagonal, 0.0)
        if version == 0:
            extra = jnp.where(lane == 1, along, jnp.where(lane == 2, energy, extra))
        blocks[pl.ds(8 * version + 7, HALF, stride=24), :] = extra


def local_part(mine, low, high, table, left_interface, right_interface):
    vmem = pl.BlockSpec(memory_space=pltpu.VMEM)
    return pl.pallas_call(
        local_kernel,
        out_shape=(
            jax.ShapeDtypeStruct((HALF * 24, W), jnp.float32),
            jax.ShapeDtypeStruct((2 * W, W), jnp.float32),
        ),
        in_specs=[vmem] * 6,
        out_specs=(vmem, vmem),
        scratch_shapes=[
            pltpu.VMEM((6, 3 * W, W), jnp.float32),
            pltpu.VMEM((8, W, 3 * W), jnp.float32),
            pltpu.VMEM((W, 3 * W), jnp.float32),
            pltpu.VMEM((2, 3 * W, 2 * W), jnp.float32),
            pltpu.VMEM((8, W, W), jnp.float32),
        ],
        name="local_part",
    )(mine, low, high, table, left_interface, right_interface)


def combine_kernel(got, out, alpha_ref, *, ranks, scale):
    parts = []
    for version in range(3):
        total = got[8 * version : 8 * version + 8]
        for source in range(1, ranks):
            total = total + got[24 * source + 8 * version : 24 * source + 8 * version + 8]
        parts.append(total)
    row, lane = iotas((8, W))
    along = jnp.sum(jnp.where((row == 7) & (lane == 1), parts[0], 0.0), keepdims=True)
    energy = jnp.sum(jnp.where((row == 7) & (lane == 2), parts[0], 0.0), keepdims=True)
    alpha = jnp.broadcast_to(along, (8, W)) / jnp.broadcast_to(energy, (8, W))
    alpha_ref[...] = alpha
    block = (parts[0] + alpha * (parts[1] + alpha * parts[2])) * scale
    for m in range(8):
        out[8 * m : 8 * m + 8] = block


def combine_part(got, ranks, scale):
    vmem = pl.BlockSpec(memory_space=pltpu.VMEM)

    def kernel(*refs):
        combine_kernel(*refs, ranks=ranks, scale=scale)

    return pl.pallas_call(
        kernel,
        out_shape=(
            jax.ShapeDtypeStruct((8 * 8, W), jnp.float32),
            jax.ShapeDtypeStruct((8, W), jnp.float32),
        ),
        in_specs=[vmem],
        out_specs=(vmem, vmem),
        name="combine_part",
    )(got)


def factor_kernel(whole, alpha_ref, mine, owned, basis, triangle, inverse, table):
    row, lane = iotas((HALF, W))
    fold = whole[pl.ds(6, HALF, stride=8), :]
    extra = whole[pl.ds(7, HALF, stride=8), :]
    under = jnp.where(lane <= row + HALF, fold, 0.0)
    upper = jnp.where((lane > row) & (lane < HALF), pltpu.roll(fold, HALF, 1), 0.0)
    upper = upper + jnp.where(lane == row, jnp.broadcast_to(extra[:, :1], (HALF, W)), 0.0)
    zero = jnp.zeros((HALF, W), jnp.float32)
    lower_part = jnp.concatenate([zero, under], axis=0)
    upper_part = jnp.concatenate([upper, zero], axis=0)
    row, lane = iotas((W, W))
    lower_part = lower_part + jnp.where(lane < row, upper_part.T, 0.0)
    table[:, :W] = lower_part.T + jnp.where(lane < row, lower_part, 0.0) + upper_part - jnp.where(
        lane > row, upper_part, 0.0
    )
    table[:, W:] = jnp.where(lane == row, 1.0, 0.0)

    sub, across = iotas((SIZE, W))
    for first in range(0, W, SIZE):
        last = first + SIZE
        panel = table[first:last, :]
        left, right = panel[:, :W], panel[:, W:]
        columns = [
            jnp.broadcast_to(left[:, first + k : first + k + 1], (SIZE, W)) for k in range(SIZE)
        ]
        for k in range(SIZE):
            pivot = jnp.broadcast_to(columns[k][k : k + 1, :], (SIZE, W))
            root = lax.rsqrt(pivot)
            root = root * (1.5 - 0.5 * pivot * (root * root))
            factor = columns[k] * root

            def eliminate(value):
                scaled = jnp.broadcast_to(value[k : k + 1, :], (SIZE, W)) * root
                return jnp.where(sub == k, scaled, jnp.where(sub > k, value - factor * scaled, value))

            left, right = eliminate(left), eliminate(right)
            for j in range(k + 1, SIZE):
                columns[j] = eliminate(columns[j])
        left = jnp.where(across >= sub + first, left, 0.0)
        triangle[first:last, :] = left
        inverse[first:last, :] = right
        if last < W:
            done = jnp.concatenate([left, right], axis=1)
            change = lax.dot_general(
                left,
                done,
                (((0,), (0,)), ((), ())),
                precision=highest,
                preferred_element_type=jnp.float32,
            )
            table[last:, :] = table[last:, :] - change[last:, :]

    alpha = alpha_ref[0:1, :]
    core = [
        mine[:, i].reshape(W, W) + alpha * owned[i * W : (i + 1) * W] for i in range(2)
    ]
    both = product(inverse[...], jnp.concatenate(core, axis=1))
    for i in range(2):
        basis[:, i] = both[:, i * W : (i + 1) * W].reshape(basis.shape[0], basis.shape[2], W)


def interface_kernel(rank, whole, inverse, out):
    rows = out.shape[1]
    start = pl.multiple_of(rank[0] * rows, rows)
    mine = inverse[pl.ds(start, rows), :]
    parts = []
    for beta in range(3):
        halves = [whole[pl.ds(2 * beta + h, HALF, stride=8), :] for h in range(2)]
        parts.append(product(mine, jnp.concatenate(halves, axis=0)))
    result = product_t(jnp.concatenate(parts, axis=0), inverse[...])
    out[...] = result.reshape(3, rows, W)


def final_part(whole, alpha, mine, owned, rank):
    vmem = pl.BlockSpec(memory_space=pltpu.VMEM)
    ranks, _, piece, _ = mine.shape
    basis, triangle, inverse = pl.pallas_call(
        factor_kernel,
        out_shape=(
            jax.ShapeDtypeStruct((ranks, 2, piece, W), jnp.float32),
            jax.ShapeDtypeStruct((W, W), jnp.float32),
            jax.ShapeDtypeStruct((W, W), jnp.float32),
        ),
        in_specs=[vmem] * 4,
        out_specs=(vmem,) * 3,
        scratch_shapes=[pltpu.VMEM((W, 2 * W), jnp.float32)],
        name="factor_part",
    )(whole, alpha, mine, owned)
    interface = pl.pallas_call(
        interface_kernel,
        out_shape=jax.ShapeDtypeStruct((3, piece, W), jnp.float32),
        in_specs=[pl.BlockSpec(memory_space=pltpu.SMEM), vmem, vmem],
        out_specs=vmem,
        name="interface_part",
    )(rank, whole, inverse)
    return basis, triangle, interface


def shards(start_core, right_side, left_interface, right_interface, couplings):
    height, piece, width = start_core.shape
    ranks = lax.axis_size("rank")
    slabs = lax.axis_size(("x", "y", "core"))
    count = slabs * ranks
    own = height // ranks
    assert width == W and own == 2 and slabs == HALF
    rank_index = lax.axis_index("rank")
    scale = 1.0 / (height * slabs * width)

    start = start_core.reshape(ranks, own, piece, width)
    right = right_side.reshape(ranks, own, piece, width)
    mine = exchange(jnp.concatenate([start, right], axis=1), "rank")

    table = lax.dynamic_slice_in_dim(couplings.reshape(27, height), rank_index * own, own, 1)
    table = jnp.pad(table, ((0, 5), (0, 0))).T[:, :, None]
    table = jnp.broadcast_to(table, (own, 32, width)).reshape(own * 32, width)
    forward = [(i, i + 1) for i in range(count - 1)]
    backward = [(target, source) for source, target in forward]

    def parcel(source, column):
        parts = [mine[:, slot].reshape(width, width) for slot in (0, 1, source)]
        return jnp.concatenate(parts + [table[32 * column : 32 * column + 32]], axis=0)

    low = lax.ppermute(parcel(3, 1), ("x", "y", "core", "rank"), forward)
    high = lax.ppermute(parcel(2, 0), ("x", "y", "core", "rank"), backward)
    blocks, owned = local_part(mine, low, high, table, left_interface, right_interface)

    block = jnp.sum(exchange(blocks.reshape(8, 192, width), ("x", "core")), axis=0)
    block = jnp.sum(exchange(block.reshape(8, 24, width), "y"), axis=0)
    block = exchange(jnp.broadcast_to(block, (ranks, 24, width)), "rank")
    block, alpha = combine_part(block.reshape(ranks * 24, width), ranks, scale)
    block = exchange(block.reshape(8, 8, width), "y").reshape(64, width)
    whole = exchange(jnp.broadcast_to(block, (8, 64, width)), ("x", "core"))

    rank = jnp.full((1,), rank_index, jnp.int32)
    basis, triangle, interface = final_part(whole.reshape(512, width), alpha, mine, owned, rank)
    output = exchange(basis, "rank").reshape(height, piece, width)
    return (output, triangle, interface)


def solution(mesh):
    names = ("x", "y", "core")
    fine = Mesh(mesh.devices.reshape(4, 8, 2, 8), names + ("rank",))
    placed = (P(names, "rank", None), P(names, "rank", None), P(), P(), P(None, None, None, names))
    return jax.shard_map(
        shards,
        mesh=fine,
        in_specs=placed,
        out_specs=(P(names, "rank", None), P(), P(None, "rank", None)),
        check_vma=False,
    )
```

```python
import jax
import jax.numpy as jnp
from jax import lax
from jax.experimental import pallas as pl
from jax.experimental.pallas import tpu as pltpu
from jax.sharding import Mesh
from jax.sharding import PartitionSpec as P

highest = lax.Precision.HIGHEST
W = 128
HALF = W // 2
SIZE = 16


def exchange(blocks, axis):
    return lax.all_to_all(blocks, axis, 0, 0, tiled=True)


def product(left, right):
    return jnp.dot(left, right, precision=highest, preferred_element_type=jnp.float32)


def product_t(left, right):
    return lax.dot_general(
        left,
        right,
        (((1,), (1,)), ((), ())),
        precision=highest,
        preferred_element_type=jnp.float32,
    )


def iotas(shape):
    return lax.broadcasted_iota(jnp.int32, shape, 0), lax.broadcasted_iota(jnp.int32, shape, 1)


def local_kernel(
    mine, low, high, ahead, behind, left_ref, right_ref, blocks, owned, terms, mixed, coupled, moved, pair
):
    def slot(index):
        return mine[:, index].reshape(W, W)

    fields = [low[0:W], low[W : 2 * W], slot(0), slot(1), high[0:W], high[W : 2 * W]]
    sources = [low[2 * W : 3 * W], slot(2), slot(3), high[2 * W : 3 * W]]
    weights = [(low, 3 * W), (behind, 3 * W), (ahead, 3 * W), (high, 3 * W)]
    right_rows = right_ref[...].reshape(3 * W, W)
    left_rows = left_ref[...].reshape(3 * W, W)
    left_lanes = jnp.concatenate([left_ref[0], left_ref[1], left_ref[2]], axis=1)

    def contract(values):
        for k in range(0, len(values), 2):
            both = product(right_rows, jnp.concatenate(values[k : k + 2], axis=1))
            terms[k] = both[:, :W]
            terms[k + 1] = both[:, W:]

    def rows_of(place):
        ref, base = place
        return [jnp.broadcast_to(ref[base + t : base + t + 1, :], (8, W)) for t in range(27)]

    def couple(place, first):
        cs = rows_of(place)

        def step(chunk, carry):
            at = pl.multiple_of(chunk * 8, 8)
            sums = [None] * 3
            for offset in range(3):
                for beta in range(3):
                    value = terms[first + offset, pl.ds(beta * W + at, 8), :]
                    for alpha in range(3):
                        part = cs[alpha * 9 + beta * 3 + offset] * value
                        sums[alpha] = part if sums[alpha] is None else sums[alpha] + part
            for alpha in range(3):
                coupled[pl.ds(at, 8), alpha * W : (alpha + 1) * W] = sums[alpha]
            return carry

        lax.fori_loop(0, W // 8, step, 0, unroll=2)
        return product_t(coupled[...], left_lanes)

    contract(fields)
    residual = [sources[i] - couple(weights[i], i) for i in range(4)]
    for i in range(4):
        pair[i] = fields[i + 1]
        pair[4 + i] = residual[i]
    owned[0:W] = residual[1]
    owned[W : 2 * W] = residual[2]
    contract(residual)
    along = jnp.zeros((1, 1), jnp.float32)
    energy = jnp.zeros((1, 1), jnp.float32)
    for i in range(2):
        image = couple(weights[1 + i], i)
        along = along + jnp.sum(pair[5 + i] * image, keepdims=True)
        energy = energy + jnp.sum(image * image, keepdims=True)

    for u in range(2):
        stack = pair[4 * u : 4 * u + 4].reshape(4 * W, W)
        mixed[4 * u : 4 * u + 4] = product_t(stack, left_rows).reshape(4, W, 3 * W)
    for i in range(2):
        cs = rows_of(weights[1 + i])

        def step(chunk, carry):
            u = chunk // (W // 8)
            at = pl.multiple_of((chunk % (W // 8)) * 8, 8)
            sums = [None] * 3
            for offset in range(3):
                for alpha in range(3):
                    value = mixed[4 * u + i + offset, pl.ds(at, 8), alpha * W : (alpha + 1) * W]
                    for beta in range(3):
                        part = cs[alpha * 9 + beta * 3 + offset] * value
                        sums[beta] = part if sums[beta] is None else sums[beta] + part
            for beta in range(3):
                moved[u, pl.ds(beta * W + at, 8), i * W : (i + 1) * W] = sums[beta]
            return carry

        lax.fori_loop(0, 2 * (W // 8), step, 0, unroll=2)

    both = jnp.concatenate(
        [
            jnp.concatenate([pair[1], pair[2]], axis=1),
            jnp.concatenate([pair[5], pair[6]], axis=1),
        ],
        axis=0,
    )
    forms = [product_t(moved[u], both) for u in range(2)]
    tables = [forms[0][:, :W], forms[0][:, W:] + forms[1][:, :W], forms[1][:, W:]]
    square = product_t(both, both)
    grams = [square[:W, :W], square[:W, W:] + square[W:, :W], square[W:, W:]]
    row, lane = iotas((HALF, W))
    for version in range(3):
        gram = grams[version]
        upper, under = gram[:HALF], gram[HALF:]
        for part in range(6):
            blocks[pl.ds(8 * version + part, HALF, stride=24), :] = tables[version][
                part * HALF : (part + 1) * HALF
            ]
        fold = jnp.where(lane <= row + HALF, under, pltpu.roll(upper, HALF, 1))
        blocks[pl.ds(8 * version + 6, HALF, stride=24), :] = fold
        diagonal = jnp.sum(jnp.where(lane == row, upper, 0.0), axis=1, keepdims=True)
        extra = jnp.where(lane == 0, diagonal, 0.0)
        if version == 0:
            extra = jnp.where(lane == 1, along, jnp.where(lane == 2, energy, extra))
        blocks[pl.ds(8 * version + 7, HALF, stride=24), :] = extra


def local_part(mine, low, high, ahead, behind, left_interface, right_interface):
    vmem = pl.BlockSpec(memory_space=pltpu.VMEM)
    return pl.pallas_call(
        local_kernel,
        out_shape=(
            jax.ShapeDtypeStruct((HALF * 24, W), jnp.float32),
            jax.ShapeDtypeStruct((2 * W, W), jnp.float32),
        ),
        in_specs=[vmem] * 7,
        out_specs=(vmem, vmem),
        scratch_shapes=[
            pltpu.VMEM((6, 3 * W, W), jnp.float32),
            pltpu.VMEM((8, W, 3 * W), jnp.float32),
            pltpu.VMEM((W, 3 * W), jnp.float32),
            pltpu.VMEM((2, 3 * W, 2 * W), jnp.float32),
            pltpu.VMEM((8, W, W), jnp.float32),
        ],
        name="local_part",
    )(mine, low, high, ahead, behind, left_interface, right_interface)


def combine_kernel(got, out, alpha_ref, *, scale):
    count = got.shape[0] // 4
    parts = [jnp.sum(got[pl.ds(v, count, stride=4), :], axis=0, keepdims=True) for v in range(4)]
    lane = lax.broadcasted_iota(jnp.int32, (1, W), 1)
    along = jnp.sum(jnp.where(lane == 1, parts[3], 0.0), axis=1, keepdims=True)
    energy = jnp.sum(jnp.where(lane == 2, parts[3], 0.0), axis=1, keepdims=True)
    alpha = jnp.broadcast_to(along, (1, W)) / jnp.broadcast_to(energy, (1, W))
    alpha_ref[...] = jnp.broadcast_to(alpha, (8, W))
    block = (parts[0] + alpha * (parts[1] + alpha * parts[2])) * scale
    out[...] = jnp.broadcast_to(block, out.shape)


def combine_part(got, scale):
    vmem = pl.BlockSpec(memory_space=pltpu.VMEM)

    def kernel(*refs):
        combine_kernel(*refs, scale=scale)

    return pl.pallas_call(
        kernel,
        out_shape=(
            jax.ShapeDtypeStruct((got.shape[0] // 4, W), jnp.float32),
            jax.ShapeDtypeStruct((8, W), jnp.float32),
        ),
        in_specs=[vmem],
        out_specs=(vmem, vmem),
        name="combine_part",
    )(got)


def factor_kernel(whole, alpha_ref, mine, owned, basis, triangle, inverse, table):
    row, lane = iotas((HALF, W))
    fold = whole[pl.ds(6, HALF, stride=8), :]
    extra = whole[pl.ds(7, HALF, stride=8), :]
    under = jnp.where(lane <= row + HALF, fold, 0.0)
    upper = jnp.where((lane > row) & (lane < HALF), pltpu.roll(fold, HALF, 1), 0.0)
    upper = upper + jnp.where(lane == row, jnp.broadcast_to(extra[:, :1], (HALF, W)), 0.0)
    zero = jnp.zeros((HALF, W), jnp.float32)
    lower_part = jnp.concatenate([zero, under], axis=0)
    upper_part = jnp.concatenate([upper, zero], axis=0)
    row, lane = iotas((W, W))
    lower_part = lower_part + jnp.where(lane < row, upper_part.T, 0.0)
    table[:, :W] = lower_part.T + jnp.where(lane < row, lower_part, 0.0) + upper_part - jnp.where(
        lane > row, upper_part, 0.0
    )
    table[:, W:] = jnp.where(lane == row, 1.0, 0.0)

    sub, across = iotas((SIZE, W))
    for first in range(0, W, SIZE):
        last = first + SIZE
        panel = table[first:last, :]
        left, right = panel[:, :W], panel[:, W:]
        columns = [
            jnp.broadcast_to(left[:, first + k : first + k + 1], (SIZE, W)) for k in range(SIZE)
        ]
        for k in range(SIZE):
            pivot = jnp.broadcast_to(columns[k][k : k + 1, :], (SIZE, W))
            root = lax.rsqrt(pivot)
            root = root * (1.5 - 0.5 * pivot * (root * root))
            factor = jnp.where(sub > k, columns[k] * (root * root), 0.0)

            def spread(value):
                return jnp.broadcast_to(value[k : k + 1, :], (SIZE, W))

            for j in range(k + 1, SIZE):
                columns[j] = columns[j] - factor * spread(columns[j])
            head = spread(left)
            left = jnp.where(sub == k, head * root, left - factor * head)
            head = spread(right)
            right = jnp.where(sub == k, head * root, right - factor * head)
        left = jnp.where(across >= sub + first, left, 0.0)
        triangle[first:last, :] = left
        inverse[first:last, :] = right
        if last < W:
            done = jnp.concatenate([left, right], axis=1)
            change = lax.dot_general(
                left,
                done,
                (((0,), (0,)), ((), ())),
                precision=highest,
                preferred_element_type=jnp.float32,
            )
            table[last:, :] = table[last:, :] - change[last:, :]

    alpha = alpha_ref[0:1, :]
    core = [
        mine[:, i].reshape(W, W) + alpha * owned[i * W : (i + 1) * W] for i in range(2)
    ]
    both = product(inverse[...], jnp.concatenate(core, axis=1))
    for i in range(2):
        basis[:, i] = both[:, i * W : (i + 1) * W].reshape(basis.shape[0], basis.shape[2], W)


def interface_kernel(rank, whole, inverse, out):
    rows = out.shape[1]
    start = pl.multiple_of(rank[0] * rows, rows)
    mine = inverse[pl.ds(start, rows), :]
    parts = []
    for beta in range(3):
        halves = [whole[pl.ds(2 * beta + h, HALF, stride=8), :] for h in range(2)]
        parts.append(product(mine, jnp.concatenate(halves, axis=0)))
    result = product_t(jnp.concatenate(parts, axis=0), inverse[...])
    out[...] = result.reshape(3, rows, W)


def final_part(whole, alpha, mine, owned, rank):
    vmem = pl.BlockSpec(memory_space=pltpu.VMEM)
    ranks, _, piece, _ = mine.shape
    basis, triangle, inverse = pl.pallas_call(
        factor_kernel,
        out_shape=(
            jax.ShapeDtypeStruct((ranks, 2, piece, W), jnp.float32),
            jax.ShapeDtypeStruct((W, W), jnp.float32),
            jax.ShapeDtypeStruct((W, W), jnp.float32),
        ),
        in_specs=[vmem] * 4,
        out_specs=(vmem,) * 3,
        scratch_shapes=[pltpu.VMEM((W, 2 * W), jnp.float32)],
        name="factor_part",
    )(whole, alpha, mine, owned)
    interface = pl.pallas_call(
        interface_kernel,
        out_shape=jax.ShapeDtypeStruct((3, piece, W), jnp.float32),
        in_specs=[pl.BlockSpec(memory_space=pltpu.SMEM), vmem, vmem],
        out_specs=vmem,
        name="interface_part",
    )(rank, whole, inverse)
    return basis, triangle, interface


def shards(start_core, right_side, left_interface, right_interface, couplings):
    height, piece, width = start_core.shape
    ranks = lax.axis_size("rank")
    slabs = lax.axis_size(("x", "y", "core"))
    count = slabs * ranks
    own = height // ranks
    assert width == W and own == 2 and slabs == HALF
    rank_index = lax.axis_index("rank")
    scale = 1.0 / (height * slabs * width)

    start = start_core.reshape(ranks, own, piece, width)
    right = right_side.reshape(ranks, own, piece, width)
    mine = exchange(jnp.concatenate([start, right], axis=1), "rank")

    table = lax.dynamic_slice_in_dim(couplings.reshape(27, height), rank_index * own, own, 1)
    table = jnp.pad(table, ((0, 5), (0, 0))).T[:, :, None]
    table = jnp.broadcast_to(table, (own, 32, width)).reshape(own * 32, width)
    forward = [(i, i + 1) for i in range(count - 1)]
    backward = [(target, source) for source, target in forward]

    def parcel(source, column):
        parts = [mine[:, slot].reshape(width, width) for slot in (0, 1, source)]
        return jnp.concatenate(parts + [table[32 * column : 32 * column + 32]], axis=0)

    ahead, behind = parcel(3, 1), parcel(2, 0)
    low = lax.ppermute(ahead, ("x", "y", "core", "rank"), forward)
    high = lax.ppermute(behind, ("x", "y", "core", "rank"), backward)
    blocks, owned = local_part(mine, low, high, ahead, behind, left_interface, right_interface)

    block = jnp.sum(exchange(blocks.reshape(8, 192, width), ("x", "core")), axis=0)
    block = block.reshape(8, 3, 8, width)
    sums = jnp.broadcast_to(block[:1, :1, 7:, :], (8, 8, 1, width))
    block = jnp.concatenate([block.transpose(0, 2, 1, 3), sums], axis=2)
    block = exchange(block.reshape(64, 4, width), ("y", "rank")).reshape(256, width)
    block, alpha = combine_part(block, scale)
    block = exchange(block.reshape(64, 1, width), ("y", "rank")).reshape(64, width)
    whole = exchange(jnp.broadcast_to(block, (8, 64, width)), ("x", "core"))

    rank = jnp.full((1,), rank_index, jnp.int32)
    basis, triangle, interface = final_part(whole.reshape(512, width), alpha, mine, owned, rank)
    output = exchange(basis, "rank").reshape(height, piece, width)
    return (output, triangle, interface)


def solution(mesh):
    names = ("x", "y", "core")
    fine = Mesh(mesh.devices.reshape(4, 8, 2, 8), names + ("rank",))
    placed = (P(names, "rank", None), P(names, "rank", None), P(), P(), P(None, None, None, names))
    return jax.shard_map(
        shards,
        mesh=fine,
        in_specs=placed,
        out_specs=(P(names, "rank", None), P(), P(None, "rank", None)),
        check_vma=False,
    )
```

```python
import jax
import jax.numpy as jnp
from jax import lax
from jax.experimental import pallas as pl
from jax.experimental.pallas import tpu as pltpu
from jax.sharding import Mesh
from jax.sharding import PartitionSpec as P

highest = lax.Precision.HIGHEST
W = 128
HALF = W // 2
SIZE = 16


def exchange(blocks, axis):
    return lax.all_to_all(blocks, axis, 0, 0, tiled=True)


def product(left, right):
    return jnp.dot(left, right, precision=highest, preferred_element_type=jnp.float32)


def product_t(left, right):
    return lax.dot_general(
        left,
        right,
        (((1,), (1,)), ((), ())),
        precision=highest,
        preferred_element_type=jnp.float32,
    )


def halves(value):
    high = value.astype(jnp.bfloat16)
    return high, (value - high.astype(jnp.float32)).astype(jnp.bfloat16)


def split_product(left, right, contract):
    def one(a, b):
        return lax.dot_general(
            a, b, (((1,), (contract,)), ((), ())), preferred_element_type=jnp.float32
        )

    return one(left[0], right[0]) + (one(left[0], right[1]) + one(left[1], right[0]))


def iotas(shape):
    return lax.broadcasted_iota(jnp.int32, shape, 0), lax.broadcasted_iota(jnp.int32, shape, 1)


def local_kernel(
    mine, low, high, ahead, behind, left_ref, right_ref, blocks, owned, terms, mixed, coupled, moved, pair
):
    def slot(index):
        return mine[:, index].reshape(W, W)

    fields = [low[0:W], low[W : 2 * W], slot(0), slot(1), high[0:W], high[W : 2 * W]]
    sources = [low[2 * W : 3 * W], slot(2), slot(3), high[2 * W : 3 * W]]
    weights = [(low, 3 * W), (behind, 3 * W), (ahead, 3 * W), (high, 3 * W)]
    right_rows = halves(right_ref[...].reshape(3 * W, W))
    left_rows = halves(left_ref[...].reshape(3 * W, W))
    left_lanes = halves(jnp.concatenate([left_ref[0], left_ref[1], left_ref[2]], axis=1))

    def contract(values):
        for k in range(0, len(values), 2):
            both = split_product(right_rows, halves(jnp.concatenate(values[k : k + 2], axis=1)), 0)
            terms[k] = both[:, :W]
            terms[k + 1] = both[:, W:]

    def rows_of(place):
        ref, base = place
        return [jnp.broadcast_to(ref[base + t : base + t + 1, :], (8, W)) for t in range(27)]

    def couple(place, first):
        cs = rows_of(place)

        def step(chunk, carry):
            at = pl.multiple_of(chunk * 8, 8)
            sums = [None] * 3
            for offset in range(3):
                for beta in range(3):
                    value = terms[first + offset, pl.ds(beta * W + at, 8), :]
                    for alpha in range(3):
                        part = cs[alpha * 9 + beta * 3 + offset] * value
                        sums[alpha] = part if sums[alpha] is None else sums[alpha] + part
            for alpha in range(3):
                coupled[pl.ds(at, 8), alpha * W : (alpha + 1) * W] = sums[alpha]
            return carry

        lax.fori_loop(0, W // 8, step, 0, unroll=2)
        return split_product(halves(coupled[...]), left_lanes, 1)

    contract(fields)
    residual = [sources[i] - couple(weights[i], i) for i in range(4)]
    for i in range(4):
        pair[i] = fields[i + 1]
        pair[4 + i] = residual[i]
    owned[0:W] = residual[1]
    owned[W : 2 * W] = residual[2]
    contract(residual)
    along = jnp.zeros((1, 1), jnp.float32)
    energy = jnp.zeros((1, 1), jnp.float32)
    for i in range(2):
        image = couple(weights[1 + i], i)
        along = along + jnp.sum(pair[5 + i] * image, keepdims=True)
        energy = energy + jnp.sum(image * image, keepdims=True)

    for u in range(2):
        stack = pair[4 * u : 4 * u + 4].reshape(4 * W, W)
        mixed[4 * u : 4 * u + 4] = split_product(halves(stack), left_rows, 1).reshape(
            4, W, 3 * W
        )
    for i in range(2):
        cs = rows_of(weights[1 + i])

        def step(chunk, carry):
            u = chunk // (W // 8)
            at = pl.multiple_of((chunk % (W // 8)) * 8, 8)
            sums = [None] * 3
            for offset in range(3):
                for alpha in range(3):
                    value = mixed[4 * u + i + offset, pl.ds(at, 8), alpha * W : (alpha + 1) * W]
                    for beta in range(3):
                        part = cs[alpha * 9 + beta * 3 + offset] * value
                        sums[beta] = part if sums[beta] is None else sums[beta] + part
            for beta in range(3):
                moved[u, pl.ds(beta * W + at, 8), i * W : (i + 1) * W] = sums[beta]
            return carry

        lax.fori_loop(0, 2 * (W // 8), step, 0, unroll=2)

    both = jnp.concatenate(
        [
            jnp.concatenate([pair[1], pair[2]], axis=1),
            jnp.concatenate([pair[5], pair[6]], axis=1),
        ],
        axis=0,
    )
    split = halves(both)
    forms = [split_product(halves(moved[u]), split, 1) for u in range(2)]
    tables = [forms[0][:, :W], forms[0][:, W:] + forms[1][:, :W], forms[1][:, W:]]
    square = product_t(both, both)
    grams = [square[:W, :W], square[:W, W:] + square[W:, :W], square[W:, W:]]
    row, lane = iotas((HALF, W))
    for version in range(3):
        gram = grams[version]
        upper, under = gram[:HALF], gram[HALF:]
        for part in range(6):
            blocks[pl.ds(8 * version + part, HALF, stride=24), :] = tables[version][
                part * HALF : (part + 1) * HALF
            ]
        fold = jnp.where(lane <= row + HALF, under, pltpu.roll(upper, HALF, 1))
        blocks[pl.ds(8 * version + 6, HALF, stride=24), :] = fold
        diagonal = jnp.sum(jnp.where(lane == row, upper, 0.0), axis=1, keepdims=True)
        extra = jnp.where(lane == 0, diagonal, 0.0)
        if version == 0:
            extra = jnp.where(lane == 1, along, jnp.where(lane == 2, energy, extra))
        blocks[pl.ds(8 * version + 7, HALF, stride=24), :] = extra


def near(*values):
    return [pltpu.with_memory_space_constraint(value, pltpu.VMEM) for value in values]


def local_part(mine, low, high, ahead, behind, left_interface, right_interface):
    vmem = pl.BlockSpec(memory_space=pltpu.VMEM)
    return pl.pallas_call(
        local_kernel,
        out_shape=(
            pltpu.VMEM((HALF * 24, W), jnp.float32),
            pltpu.VMEM((2 * W, W), jnp.float32),
        ),
        in_specs=[vmem] * 7,
        out_specs=(vmem, vmem),
        scratch_shapes=[
            pltpu.VMEM((6, 3 * W, W), jnp.float32),
            pltpu.VMEM((8, W, 3 * W), jnp.float32),
            pltpu.VMEM((W, 3 * W), jnp.float32),
            pltpu.VMEM((2, 3 * W, 2 * W), jnp.float32),
            pltpu.VMEM((8, W, W), jnp.float32),
        ],
        name="local_part",
    )(*near(mine, low, high, ahead, behind), left_interface, right_interface)


def combine_kernel(got, out, alpha_ref, *, scale):
    count = got.shape[0] // 4
    parts = [jnp.sum(got[pl.ds(v, count, stride=4), :], axis=0, keepdims=True) for v in range(4)]
    lane = lax.broadcasted_iota(jnp.int32, (1, W), 1)
    along = jnp.sum(jnp.where(lane == 1, parts[3], 0.0), axis=1, keepdims=True)
    energy = jnp.sum(jnp.where(lane == 2, parts[3], 0.0), axis=1, keepdims=True)
    alpha = jnp.broadcast_to(along, (1, W)) / jnp.broadcast_to(energy, (1, W))
    alpha_ref[...] = jnp.broadcast_to(alpha, (8, W))
    block = (parts[0] + alpha * (parts[1] + alpha * parts[2])) * scale
    out[...] = jnp.broadcast_to(block, out.shape)


def combine_part(got, scale):
    vmem = pl.BlockSpec(memory_space=pltpu.VMEM)

    def kernel(*refs):
        combine_kernel(*refs, scale=scale)

    return pl.pallas_call(
        kernel,
        out_shape=(
            pltpu.VMEM((got.shape[0] // 4, W), jnp.float32),
            pltpu.VMEM((8, W), jnp.float32),
        ),
        in_specs=[vmem],
        out_specs=(vmem, vmem),
        name="combine_part",
    )(*near(got))


def factor_kernel(whole, alpha_ref, mine, owned, basis, triangle, inverse, table):
    row, lane = iotas((HALF, W))
    fold = whole[pl.ds(6, HALF, stride=8), :]
    extra = whole[pl.ds(7, HALF, stride=8), :]
    under = jnp.where(lane <= row + HALF, fold, 0.0)
    upper = jnp.where((lane > row) & (lane < HALF), pltpu.roll(fold, HALF, 1), 0.0)
    upper = upper + jnp.where(lane == row, jnp.broadcast_to(extra[:, :1], (HALF, W)), 0.0)
    zero = jnp.zeros((HALF, W), jnp.float32)
    lower_part = jnp.concatenate([zero, under], axis=0)
    upper_part = jnp.concatenate([upper, zero], axis=0)
    row, lane = iotas((W, W))
    lower_part = lower_part + jnp.where(lane < row, upper_part.T, 0.0)
    table[:, :W] = lower_part.T + jnp.where(lane < row, lower_part, 0.0) + upper_part - jnp.where(
        lane > row, upper_part, 0.0
    )
    table[:, W:] = jnp.where(lane == row, 1.0, 0.0)

    sub, across = iotas((SIZE, W))
    for first in range(0, W, SIZE):
        last = first + SIZE
        panel = table[first:last, :]
        left, right = panel[:, :W], panel[:, W:]
        columns = [
            jnp.broadcast_to(left[:, first + k : first + k + 1], (SIZE, W)) for k in range(SIZE)
        ]
        for k in range(SIZE):
            pivot = jnp.broadcast_to(columns[k][k : k + 1, :], (SIZE, W))
            root = lax.rsqrt(pivot)
            root = root * (1.5 - 0.5 * pivot * (root * root))
            factor = jnp.where(sub > k, columns[k] * (root * root), 0.0)

            def spread(value):
                return jnp.broadcast_to(value[k : k + 1, :], (SIZE, W))

            for j in range(k + 1, SIZE):
                columns[j] = columns[j] - factor * spread(columns[j])
            head = spread(left)
            left = jnp.where(sub == k, head * root, left - factor * head)
            head = spread(right)
            right = jnp.where(sub == k, head * root, right - factor * head)
        left = jnp.where(across >= sub + first, left, 0.0)
        triangle[first:last, :] = left
        inverse[first:last, :] = right
        if last < W:
            done = jnp.concatenate([left, right], axis=1)
            change = lax.dot_general(
                left,
                done,
                (((0,), (0,)), ((), ())),
                precision=highest,
                preferred_element_type=jnp.float32,
            )
            table[last:, :] = table[last:, :] - change[last:, :]

    alpha = alpha_ref[0:1, :]
    core = [
        mine[:, i].reshape(W, W) + alpha * owned[i * W : (i + 1) * W] for i in range(2)
    ]
    both = product(inverse[...], jnp.concatenate(core, axis=1))
    for i in range(2):
        basis[:, i] = both[:, i * W : (i + 1) * W].reshape(basis.shape[0], basis.shape[2], W)


def interface_kernel(rank, whole, inverse, out):
    rows = out.shape[1]
    start = pl.multiple_of(rank[0] * rows, rows)
    mine = inverse[pl.ds(start, rows), :]
    parts = []
    for beta in range(3):
        halves = [whole[pl.ds(2 * beta + h, HALF, stride=8), :] for h in range(2)]
        parts.append(product(mine, jnp.concatenate(halves, axis=0)))
    result = product_t(jnp.concatenate(parts, axis=0), inverse[...])
    out[...] = result.reshape(3, rows, W)


def final_part(whole, alpha, mine, owned, rank):
    vmem = pl.BlockSpec(memory_space=pltpu.VMEM)
    ranks, _, piece, _ = mine.shape
    basis, triangle, inverse = pl.pallas_call(
        factor_kernel,
        out_shape=(
            pltpu.VMEM((ranks, 2, piece, W), jnp.float32),
            jax.ShapeDtypeStruct((W, W), jnp.float32),
            pltpu.VMEM((W, W), jnp.float32),
        ),
        in_specs=[vmem] * 4,
        out_specs=(vmem,) * 3,
        scratch_shapes=[pltpu.VMEM((W, 2 * W), jnp.float32)],
        name="factor_part",
    )(*near(whole, alpha, mine, owned))
    interface = pl.pallas_call(
        interface_kernel,
        out_shape=jax.ShapeDtypeStruct((3, piece, W), jnp.float32),
        in_specs=[pl.BlockSpec(memory_space=pltpu.SMEM), vmem, vmem],
        out_specs=vmem,
        name="interface_part",
    )(rank, *near(whole, inverse))
    return basis, triangle, interface


def shards(start_core, right_side, left_interface, right_interface, couplings):
    height, piece, width = start_core.shape
    ranks = lax.axis_size("rank")
    slabs = lax.axis_size(("x", "y", "core"))
    count = slabs * ranks
    own = height // ranks
    assert width == W and own == 2 and slabs == HALF
    rank_index = lax.axis_index("rank")
    scale = 1.0 / (height * slabs * width)

    start = start_core.reshape(ranks, own, piece, width)
    right = right_side.reshape(ranks, own, piece, width)
    mine = exchange(jnp.concatenate([start, right], axis=1), "rank")

    table = lax.dynamic_slice_in_dim(couplings.reshape(27, height), rank_index * own, own, 1)
    table = jnp.pad(table, ((0, 5), (0, 0))).T[:, :, None]
    table = jnp.broadcast_to(table, (own, 32, width)).reshape(own * 32, width)
    forward = [(i, i + 1) for i in range(count - 1)]
    backward = [(target, source) for source, target in forward]

    def parcel(source, column):
        parts = [mine[:, slot].reshape(width, width) for slot in (0, 1, source)]
        return jnp.concatenate(parts + [table[32 * column : 32 * column + 32]], axis=0)

    ahead, behind = parcel(3, 1), parcel(2, 0)
    low = lax.ppermute(ahead, ("x", "y", "core", "rank"), forward)
    high = lax.ppermute(behind, ("x", "y", "core", "rank"), backward)
    blocks, owned = local_part(mine, low, high, ahead, behind, left_interface, right_interface)

    block = jnp.sum(exchange(blocks.reshape(8, 192, width), ("x", "core")), axis=0)
    block = block.reshape(8, 3, 8, width)
    sums = jnp.broadcast_to(block[:1, :1, 7:, :], (8, 8, 1, width))
    block = jnp.concatenate([block.transpose(0, 2, 1, 3), sums], axis=2)
    block = exchange(block.reshape(64, 4, width), ("y", "rank")).reshape(256, width)
    block, alpha = combine_part(block, scale)
    block = exchange(block.reshape(64, 1, width), ("y", "rank")).reshape(64, width)
    whole = exchange(jnp.broadcast_to(block, (8, 64, width)), ("x", "core"))

    rank = jnp.full((1,), rank_index, jnp.int32)
    basis, triangle, interface = final_part(whole.reshape(512, width), alpha, mine, owned, rank)
    output = exchange(basis, "rank").reshape(height, piece, width)
    return (output, triangle, interface)


def solution(mesh):
    names = ("x", "y", "core")
    fine = Mesh(mesh.devices.reshape(4, 8, 2, 8), names + ("rank",))
    placed = (P(names, "rank", None), P(names, "rank", None), P(), P(), P(None, None, None, names))
    return jax.shard_map(
        shards,
        mesh=fine,
        in_specs=placed,
        out_specs=(P(names, "rank", None), P(), P(None, "rank", None)),
        check_vma=False,
    )
```

```python
import jax
import jax.numpy as jnp
from jax import lax
from jax.experimental import pallas as pl
from jax.experimental.pallas import tpu as pltpu
from jax.sharding import Mesh
from jax.sharding import PartitionSpec as P

highest = lax.Precision.HIGHEST
W = 128
HALF = W // 2
SIZE = 16
ROOM = 16 * 2**20


def exchange(blocks, axis):
    return lax.all_to_all(blocks, axis, 0, 0, tiled=True)


def product(left, right):
    return jnp.dot(left, right, precision=highest, preferred_element_type=jnp.float32)


def product_t(left, right):
    return lax.dot_general(
        left,
        right,
        (((1,), (1,)), ((), ())),
        precision=highest,
        preferred_element_type=jnp.float32,
    )


def halves(value):
    high = value.astype(jnp.bfloat16)
    return high, (value - high.astype(jnp.float32)).astype(jnp.bfloat16)


def split_product(left, right, contract):
    def one(a, b):
        return lax.dot_general(
            a, b, (((1,), (contract,)), ((), ())), preferred_element_type=jnp.float32
        )

    return one(left[0], right[0]) + (one(left[0], right[1]) + one(left[1], right[0]))


def iotas(shape):
    return lax.broadcasted_iota(jnp.int32, shape, 0), lax.broadcasted_iota(jnp.int32, shape, 1)


def near(*values):
    return [pltpu.with_memory_space_constraint(value, pltpu.VMEM) for value in values]


def own_slot(mine, index):
    return mine[:, index].reshape(W, W)


def contract(right_rows, values, terms, first):
    for k in range(0, len(values), 2):
        both = split_product(right_rows, halves(jnp.concatenate(values[k : k + 2], axis=1)), 0)
        terms[first + k] = both[:, :W]
        terms[first + k + 1] = both[:, W:]


def couple(place, sources, target, base, left_first):
    ref, start = place
    used = {offset for offset, _ in sources}
    weight = {
        (i, j, offset): jnp.broadcast_to(
            ref[start + i * 9 + j * 3 + offset : start + i * 9 + j * 3 + offset + 1, :], (8, W)
        )
        for i in range(3)
        for j in range(3)
        for offset in used
    }

    def step(chunk, carry):
        at = pl.multiple_of(chunk * 8, 8)
        sums = [None if base is None else base(index, at) for index in range(3)]
        for offset, rows in sources:
            for inner in range(3):
                value = rows(inner, at)
                for outer in range(3):
                    key = (inner, outer) if left_first else (outer, inner)
                    part = weight[key + (offset,)] * value
                    sums[outer] = part if sums[outer] is None else sums[outer] + part
        for index in range(3):
            target(index, at, sums[index])
        return carry

    lax.fori_loop(0, W // 8, step, 0, unroll=2)


def term_rows(terms, place):
    return lambda index, at: terms[place, pl.ds(index * W + at, 8), :]


def mixed_rows(mixed, place):
    return lambda index, at: mixed[place, pl.ds(at, 8), index * W : (index + 1) * W]


def lanes_of(ref, place):
    def load(index, at):
        return ref[place, pl.ds(at, 8), index * W : (index + 1) * W]

    def store(index, at, value):
        ref[place, pl.ds(at, 8), index * W : (index + 1) * W] = value

    return load, store


def moved_of(ref, lead, place):
    def load(index, at):
        return ref[lead + (pl.ds(index * W + at, 8), slice(place * W, (place + 1) * W))]

    def store(index, at, value):
        ref[lead + (pl.ds(index * W + at, 8), slice(place * W, (place + 1) * W))] = value

    return load, store


def early_kernel(mine, ahead, behind, left_ref, right_ref, terms, partial, shifted, mixed):
    right_rows = halves(right_ref[...].reshape(3 * W, W))
    left_rows = halves(left_ref[...].reshape(3 * W, W))
    fields = [own_slot(mine, 0), own_slot(mine, 1)]
    weights = [(behind, 3 * W), (ahead, 3 * W)]
    contract(right_rows, fields, terms, 0)
    stack = halves(jnp.concatenate(fields, axis=0))
    mixed[...] = split_product(stack, left_rows, 1).reshape(2, W, 3 * W)
    for i in range(2):
        present = [(1 - i + k, term_rows(terms, k)) for k in range(2)]
        couple(weights[i], present, lanes_of(partial, i)[1], None, False)
        present = [(1 - i + k, mixed_rows(mixed, k)) for k in range(2)]
        couple(weights[i], present, moved_of(shifted, (), i)[1], None, True)


def early_part(mine, ahead, behind, left_interface, right_interface):
    vmem = pl.BlockSpec(memory_space=pltpu.VMEM)
    return pl.pallas_call(
        early_kernel,
        out_shape=(
            pltpu.VMEM((2, 3 * W, W), jnp.float32),
            pltpu.VMEM((2, W, 3 * W), jnp.float32),
            pltpu.VMEM((3 * W, 2 * W), jnp.float32),
        ),
        in_specs=[vmem] * 5,
        out_specs=(vmem,) * 3,
        scratch_shapes=[pltpu.VMEM((2, W, 3 * W), jnp.float32)],
        compiler_params=pltpu.CompilerParams(vmem_limit_bytes=ROOM),
        name="early_part",
    )(*near(mine, ahead, behind, left_interface, right_interface))


def local_kernel(
    mine,
    low,
    high,
    ahead,
    behind,
    own_terms,
    partial,
    shifted,
    left_ref,
    right_ref,
    blocks,
    owned,
    terms,
    mixed,
    coupled,
    moved,
    pair,
):
    outer = [low[0:W], low[W : 2 * W], high[0:W], high[W : 2 * W]]
    sources = [low[2 * W : 3 * W], own_slot(mine, 2), own_slot(mine, 3), high[2 * W : 3 * W]]
    weights = [(low, 3 * W), (behind, 3 * W), (ahead, 3 * W), (high, 3 * W)]
    right_rows = halves(right_ref[...].reshape(3 * W, W))
    left_rows = halves(left_ref[...].reshape(3 * W, W))
    left_lanes = halves(jnp.concatenate([left_ref[0], left_ref[1], left_ref[2]], axis=1))
    store = lanes_of(coupled, 0)[1]

    def finish():
        return split_product(halves(coupled[0]), left_lanes, 1)

    contract(right_rows, outer, terms, 0)
    lists = [
        [(0, term_rows(terms, 0)), (1, term_rows(terms, 1)), (2, term_rows(own_terms, 0))],
        [(0, term_rows(terms, 1))],
        [(2, term_rows(terms, 2))],
        [(0, term_rows(own_terms, 1)), (1, term_rows(terms, 2)), (2, term_rows(terms, 3))],
    ]
    residual = []
    for i in range(4):
        base = lanes_of(partial, i - 1)[0] if i in (1, 2) else None
        couple(weights[i], lists[i], store, base, False)
        residual.append(sources[i] - finish())
    pair[0], pair[3] = outer[1], outer[2]
    pair[1], pair[2] = own_slot(mine, 0), own_slot(mine, 1)
    for i in range(4):
        pair[4 + i] = residual[i]
    owned[0:W] = residual[1]
    owned[W : 2 * W] = residual[2]
    contract(right_rows, residual, terms, 0)
    along = jnp.zeros((1, 1), jnp.float32)
    energy = jnp.zeros((1, 1), jnp.float32)
    for i in range(2):
        present = [(offset, term_rows(terms, i + offset)) for offset in range(3)]
        couple(weights[1 + i], present, store, None, False)
        image = finish()
        along = along + jnp.sum(pair[5 + i] * image, keepdims=True)
        energy = energy + jnp.sum(image * image, keepdims=True)

    stack = halves(jnp.concatenate([outer[1], outer[2]] + residual, axis=0))
    mixed[...] = split_product(stack, left_rows, 1).reshape(6, W, 3 * W)
    for i in range(2):
        base = moved_of(shifted, (), i)[0]
        present = [(2 * i, mixed_rows(mixed, i))]
        couple(weights[1 + i], present, moved_of(moved, (0,), i)[1], base, True)
        present = [(offset, mixed_rows(mixed, 2 + i + offset)) for offset in range(3)]
        couple(weights[1 + i], present, moved_of(moved, (1,), i)[1], None, True)

    both = jnp.concatenate(
        [
            jnp.concatenate([pair[1], pair[2]], axis=1),
            jnp.concatenate([pair[5], pair[6]], axis=1),
        ],
        axis=0,
    )
    split = halves(both)
    forms = [split_product(halves(moved[u]), split, 1) for u in range(2)]
    tables = [forms[0][:, :W], forms[0][:, W:] + forms[1][:, :W], forms[1][:, W:]]
    square = product_t(both, both)
    grams = [square[:W, :W], square[:W, W:] + square[W:, :W], square[W:, W:]]
    row, lane = iotas((HALF, W))
    for version in range(3):
        gram = grams[version]
        upper, under = gram[:HALF], gram[HALF:]
        for part in range(6):
            blocks[pl.ds(8 * version + part, HALF, stride=24), :] = tables[version][
                part * HALF : (part + 1) * HALF
            ]
        fold = jnp.where(lane <= row + HALF, under, pltpu.roll(upper, HALF, 1))
        blocks[pl.ds(8 * version + 6, HALF, stride=24), :] = fold
        diagonal = jnp.sum(jnp.where(lane == row, upper, 0.0), axis=1, keepdims=True)
        extra = jnp.where(lane == 0, diagonal, 0.0)
        if version == 0:
            extra = jnp.where(lane == 1, along, jnp.where(lane == 2, energy, extra))
        blocks[pl.ds(8 * version + 7, HALF, stride=24), :] = extra


def local_part(mine, low, high, ahead, behind, early, left_interface, right_interface):
    vmem = pl.BlockSpec(memory_space=pltpu.VMEM)
    return pl.pallas_call(
        local_kernel,
        out_shape=(
            pltpu.VMEM((HALF * 24, W), jnp.float32),
            pltpu.VMEM((2 * W, W), jnp.float32),
        ),
        in_specs=[vmem] * 10,
        out_specs=(vmem, vmem),
        scratch_shapes=[
            pltpu.VMEM((4, 3 * W, W), jnp.float32),
            pltpu.VMEM((6, W, 3 * W), jnp.float32),
            pltpu.VMEM((1, W, 3 * W), jnp.float32),
            pltpu.VMEM((2, 3 * W, 2 * W), jnp.float32),
            pltpu.VMEM((8, W, W), jnp.float32),
        ],
        compiler_params=pltpu.CompilerParams(vmem_limit_bytes=ROOM),
        name="local_part",
    )(*near(mine, low, high, ahead, behind, *early, left_interface, right_interface))


def combine_kernel(got, out, alpha_ref, *, scale):
    count = got.shape[0] // 4
    parts = [jnp.sum(got[pl.ds(v, count, stride=4), :], axis=0, keepdims=True) for v in range(4)]
    lane = lax.broadcasted_iota(jnp.int32, (1, W), 1)
    along = jnp.sum(jnp.where(lane == 1, parts[3], 0.0), axis=1, keepdims=True)
    energy = jnp.sum(jnp.where(lane == 2, parts[3], 0.0), axis=1, keepdims=True)
    alpha = jnp.broadcast_to(along, (1, W)) / jnp.broadcast_to(energy, (1, W))
    alpha_ref[...] = jnp.broadcast_to(alpha, (8, W))
    block = (parts[0] + alpha * (parts[1] + alpha * parts[2])) * scale
    out[...] = jnp.broadcast_to(block, out.shape)


def combine_part(got, scale):
    vmem = pl.BlockSpec(memory_space=pltpu.VMEM)

    def kernel(*refs):
        combine_kernel(*refs, scale=scale)

    return pl.pallas_call(
        kernel,
        out_shape=(
            pltpu.VMEM((got.shape[0] // 4, W), jnp.float32),
            pltpu.VMEM((8, W), jnp.float32),
        ),
        in_specs=[vmem],
        out_specs=(vmem, vmem),
        compiler_params=pltpu.CompilerParams(vmem_limit_bytes=ROOM),
        name="combine_part",
    )(*near(got))


def factor_kernel(whole, alpha_ref, mine, owned, basis, triangle, inverse, table):
    row, lane = iotas((HALF, W))
    fold = whole[pl.ds(6, HALF, stride=8), :]
    extra = whole[pl.ds(7, HALF, stride=8), :]
    under = jnp.where(lane <= row + HALF, fold, 0.0)
    upper = jnp.where((lane > row) & (lane < HALF), pltpu.roll(fold, HALF, 1), 0.0)
    upper = upper + jnp.where(lane == row, jnp.broadcast_to(extra[:, :1], (HALF, W)), 0.0)
    zero = jnp.zeros((HALF, W), jnp.float32)
    lower_part = jnp.concatenate([zero, under], axis=0)
    upper_part = jnp.concatenate([upper, zero], axis=0)
    row, lane = iotas((W, W))
    lower_part = lower_part + jnp.where(lane < row, upper_part.T, 0.0)
    table[:, :W] = lower_part.T + jnp.where(lane < row, lower_part, 0.0) + upper_part - jnp.where(
        lane > row, upper_part, 0.0
    )
    table[:, W:] = jnp.where(lane == row, 1.0, 0.0)

    sub, across = iotas((SIZE, W))
    for first in range(0, W, SIZE):
        last = first + SIZE
        panel = table[first:last, :]
        left, right = panel[:, :W], panel[:, W:]
        columns = [
            jnp.broadcast_to(left[:, first + k : first + k + 1], (SIZE, W)) for k in range(SIZE)
        ]
        for k in range(SIZE):
            pivot = jnp.broadcast_to(columns[k][k : k + 1, :], (SIZE, W))
            root = lax.rsqrt(pivot)
            root = root * (1.5 - 0.5 * pivot * (root * root))
            factor = jnp.where(sub > k, columns[k] * (root * root), 0.0)

            def spread(value):
                return jnp.broadcast_to(value[k : k + 1, :], (SIZE, W))

            for j in range(k + 1, SIZE):
                columns[j] = columns[j] - factor * spread(columns[j])
            head = spread(left)
            left = jnp.where(sub == k, head * root, left - factor * head)
            head = spread(right)
            right = jnp.where(sub == k, head * root, right - factor * head)
        left = jnp.where(across >= sub + first, left, 0.0)
        triangle[first:last, :] = left
        inverse[first:last, :] = right
        if last < W:
            done = jnp.concatenate([left, right], axis=1)
            turned = left.T
            for low, high in ((last, last + SIZE), (last + SIZE, W)):
                if low < high:
                    table[low:high, :] = table[low:high, :] - product(turned[low:high], done)

    alpha = alpha_ref[0:1, :]
    core = [
        mine[:, i].reshape(W, W) + alpha * owned[i * W : (i + 1) * W] for i in range(2)
    ]
    both = product(inverse[...], jnp.concatenate(core, axis=1))
    for i in range(2):
        basis[:, i] = both[:, i * W : (i + 1) * W].reshape(basis.shape[0], basis.shape[2], W)


def interface_kernel(rank, whole, inverse, out):
    rows = out.shape[1]
    start = pl.multiple_of(rank[0] * rows, rows)
    mine = inverse[pl.ds(start, rows), :]
    parts = []
    for beta in range(3):
        halves = [whole[pl.ds(2 * beta + h, HALF, stride=8), :] for h in range(2)]
        parts.append(product(mine, jnp.concatenate(halves, axis=0)))
    result = product_t(jnp.concatenate(parts, axis=0), inverse[...])
    out[...] = result.reshape(3, rows, W)


def final_part(whole, alpha, mine, owned, rank):
    vmem = pl.BlockSpec(memory_space=pltpu.VMEM)
    ranks, _, piece, _ = mine.shape
    basis, triangle, inverse = pl.pallas_call(
        factor_kernel,
        out_shape=(
            pltpu.VMEM((ranks, 2, piece, W), jnp.float32),
            jax.ShapeDtypeStruct((W, W), jnp.float32),
            pltpu.VMEM((W, W), jnp.float32),
        ),
        in_specs=[vmem] * 4,
        out_specs=(vmem,) * 3,
        scratch_shapes=[pltpu.VMEM((W, 2 * W), jnp.float32)],
        compiler_params=pltpu.CompilerParams(vmem_limit_bytes=ROOM),
        name="factor_part",
    )(*near(whole, alpha, mine, owned))
    interface = pl.pallas_call(
        interface_kernel,
        out_shape=jax.ShapeDtypeStruct((3, piece, W), jnp.float32),
        in_specs=[pl.BlockSpec(memory_space=pltpu.SMEM), vmem, vmem],
        out_specs=vmem,
        compiler_params=pltpu.CompilerParams(vmem_limit_bytes=ROOM),
        name="interface_part",
    )(rank, *near(whole, inverse))
    return basis, triangle, interface


def shards(start_core, right_side, left_interface, right_interface, couplings):
    height, piece, width = start_core.shape
    ranks = lax.axis_size("rank")
    slabs = lax.axis_size(("x", "y", "core"))
    count = slabs * ranks
    own = height // ranks
    assert width == W and own == 2 and slabs == HALF
    rank_index = lax.axis_index("rank")
    scale = 1.0 / (height * slabs * width)

    start = start_core.reshape(ranks, own, piece, width)
    right = right_side.reshape(ranks, own, piece, width)
    mine = exchange(jnp.concatenate([start, right], axis=1), "rank")

    table = lax.dynamic_slice_in_dim(couplings.reshape(27, height), rank_index * own, own, 1)
    table = jnp.pad(table, ((0, 5), (0, 0))).T[:, :, None]
    table = jnp.broadcast_to(table, (own, 32, width)).reshape(own * 32, width)
    forward = [(i, i + 1) for i in range(count - 1)]
    backward = [(target, source) for source, target in forward]

    def parcel(source, column):
        parts = [mine[:, slot].reshape(width, width) for slot in (0, 1, source)]
        return jnp.concatenate(parts + [table[32 * column : 32 * column + 32]], axis=0)

    ahead, behind = parcel(3, 1), parcel(2, 0)
    low = lax.ppermute(ahead, ("x", "y", "core", "rank"), forward)
    high = lax.ppermute(behind, ("x", "y", "core", "rank"), backward)
    early = early_part(mine, ahead, behind, left_interface, right_interface)
    blocks, owned = local_part(
        mine, low, high, ahead, behind, early, left_interface, right_interface
    )

    block = jnp.sum(exchange(blocks.reshape(8, 192, width), ("x", "core")), axis=0)
    block = block.reshape(8, 3, 8, width)
    sums = jnp.broadcast_to(block[:1, :1, 7:, :], (8, 8, 1, width))
    block = jnp.concatenate([block.transpose(0, 2, 1, 3), sums], axis=2)
    block = exchange(block.reshape(64, 4, width), ("y", "rank")).reshape(256, width)
    block, alpha = combine_part(block, scale)
    block = exchange(block.reshape(64, 1, width), ("y", "rank")).reshape(64, width)
    whole = exchange(jnp.broadcast_to(block, (8, 64, width)), ("x", "core"))

    rank = jnp.full((1,), rank_index, jnp.int32)
    basis, triangle, interface = final_part(whole.reshape(512, width), alpha, mine, owned, rank)
    output = exchange(basis, "rank").reshape(height, piece, width)
    return (output, triangle, interface)


def solution(mesh):
    names = ("x", "y", "core")
    fine = Mesh(mesh.devices.reshape(4, 8, 2, 8), names + ("rank",))
    placed = (P(names, "rank", None), P(names, "rank", None), P(), P(), P(None, None, None, names))
    return jax.shard_map(
        shards,
        mesh=fine,
        in_specs=placed,
        out_specs=(P(names, "rank", None), P(), P(None, "rank", None)),
        check_vma=False,
    )
```

```python
import jax
import jax.numpy as jnp
from jax import lax
from jax.experimental import pallas as pl
from jax.experimental.pallas import tpu as pltpu
from jax.sharding import Mesh
from jax.sharding import PartitionSpec as P

highest = lax.Precision.HIGHEST
W = 128
HALF = W // 2
SIZE = 16
ROOM = 16 * 2**20


def exchange(blocks, axis):
    return lax.all_to_all(blocks, axis, 0, 0, tiled=True)


def product(left, right):
    return jnp.dot(left, right, precision=highest, preferred_element_type=jnp.float32)


def product_t(left, right):
    return lax.dot_general(
        left,
        right,
        (((1,), (1,)), ((), ())),
        precision=highest,
        preferred_element_type=jnp.float32,
    )


def halves(value):
    high = value.astype(jnp.bfloat16)
    return high, (value - high.astype(jnp.float32)).astype(jnp.bfloat16)


def split_product(left, right, contract):
    def one(a, b):
        return lax.dot_general(
            a, b, (((1,), (contract,)), ((), ())), preferred_element_type=jnp.float32
        )

    return one(left[0], right[0]) + (one(left[0], right[1]) + one(left[1], right[0]))


def iotas(shape):
    return lax.broadcasted_iota(jnp.int32, shape, 0), lax.broadcasted_iota(jnp.int32, shape, 1)


def near(*values):
    return [pltpu.with_memory_space_constraint(value, pltpu.VMEM) for value in values]


def pack_kernel(start, right, packed, done):
    copies = []
    for field, ref in enumerate((start, right)):
        for half in range(2):
            part = pl.ds(half * (ref.shape[0] // 2), ref.shape[0] // 2)
            copies.append(
                pltpu.make_async_copy(
                    ref.at[part], packed.at[part, pl.ds(2 * field, 2)], done.at[2 * field + half]
                )
            )
    for copy in copies:
        copy.start()
    for copy in copies:
        copy.wait()


def pack_part(start, right):
    anywhere = pl.BlockSpec(memory_space=pltpu.HBM)
    ranks, _, piece, _ = start.shape
    return pl.pallas_call(
        pack_kernel,
        out_shape=jax.ShapeDtypeStruct((ranks, 4, piece, W), jnp.float32),
        in_specs=[anywhere] * 2,
        out_specs=anywhere,
        scratch_shapes=[pltpu.SemaphoreType.DMA((4,))],
        compiler_params=pltpu.CompilerParams(vmem_limit_bytes=ROOM),
        name="pack_part",
    )(*(pltpu.with_memory_space_constraint(value, pltpu.HBM) for value in (start, right)))


def own_slot(mine, index):
    return mine[:, index].reshape(W, W)


def contract(right_rows, values, terms, first):
    for k in range(0, len(values), 2):
        both = split_product(right_rows, halves(jnp.concatenate(values[k : k + 2], axis=1)), 0)
        terms[first + k] = both[:, :W]
        terms[first + k + 1] = both[:, W:]


def couple(place, sources, target, base, left_first):
    used = {offset for offset, _ in sources}
    weight = {
        (i, j, offset): jnp.broadcast_to(place(i, j, offset), (8, W))
        for i in range(3)
        for j in range(3)
        for offset in used
    }

    def step(chunk, carry):
        at = pl.multiple_of(chunk * 8, 8)
        sums = [None if base is None else base(index, at) for index in range(3)]
        for offset, rows in sources:
            for inner in range(3):
                value = rows(inner, at)
                for outer in range(3):
                    key = (inner, outer) if left_first else (outer, inner)
                    part = weight[key + (offset,)] * value
                    sums[outer] = part if sums[outer] is None else sums[outer] + part
        for index in range(3):
            target(index, at, sums[index])
        return carry

    lax.fori_loop(0, W // 8, step, 0, unroll=2)


def term_rows(terms, place):
    return lambda index, at: terms[place, pl.ds(index * W + at, 8), :]


def mixed_rows(mixed, place):
    return lambda index, at: mixed[place, pl.ds(at, 8), index * W : (index + 1) * W]


def lanes_of(ref, place):
    def load(index, at):
        return ref[place, pl.ds(at, 8), index * W : (index + 1) * W]

    def store(index, at, value):
        ref[place, pl.ds(at, 8), index * W : (index + 1) * W] = value

    return load, store


def moved_of(ref, lead, place):
    def load(index, at):
        return ref[lead + (pl.ds(index * W + at, 8), slice(place * W, (place + 1) * W))]

    def store(index, at, value):
        ref[lead + (pl.ds(index * W + at, 8), slice(place * W, (place + 1) * W))] = value

    return load, store


def own_row(table, mode):
    def row(i, j, offset):
        at = 32 * mode + 9 * i + 3 * j + offset
        return table[at : at + 1, :]

    return row


def sent_row(parcel):
    return lambda i, j, offset: parcel[2 * W + 3 * i + j : 2 * W + 3 * i + j + 1, :]


def parcel_kernel(mine, table, left_ref, right_ref, ahead, behind, terms, coupled):
    right_rows = halves(right_ref[...].reshape(3 * W, W))
    left_lanes = halves(jnp.concatenate([left_ref[0], left_ref[1], left_ref[2]], axis=1))
    contract(right_rows, [own_slot(mine, 0), own_slot(mine, 1)], terms, 0)
    for i in range(2):
        present = [(1 - i + k, term_rows(terms, k)) for k in range(2)]
        couple(own_row(table, i), present, lanes_of(coupled, i)[1], None, False)
    applied = split_product(halves(coupled[...].reshape(2 * W, 3 * W)), left_lanes, 1)
    for i, parcel, offset in ((0, behind, 0), (1, ahead, 2)):
        parcel[0:W] = own_slot(mine, i)
        parcel[W : 2 * W] = own_slot(mine, 2 + i) - applied[i * W : (i + 1) * W]
        parcel[2 * W : 2 * W + 16] = jnp.zeros((16, W), jnp.float32)
        row = own_row(table, i)
        for alpha in range(3):
            for beta in range(3):
                at = 2 * W + 3 * alpha + beta
                parcel[at : at + 1, :] = row(alpha, beta, offset)


def parcel_part(mine, table, left_interface, right_interface):
    vmem = pl.BlockSpec(memory_space=pltpu.VMEM)
    return pl.pallas_call(
        parcel_kernel,
        out_shape=(
            pltpu.VMEM((2 * W + 16, W), jnp.float32),
            pltpu.VMEM((2 * W + 16, W), jnp.float32),
            pltpu.VMEM((2, 3 * W, W), jnp.float32),
        ),
        in_specs=[vmem] * 4,
        out_specs=(vmem,) * 3,
        scratch_shapes=[pltpu.VMEM((2, W, 3 * W), jnp.float32)],
        compiler_params=pltpu.CompilerParams(vmem_limit_bytes=ROOM),
        name="parcel_part",
    )(*near(mine, table, left_interface, right_interface))


def early_kernel(mine, table, left_ref, shifted, mixed):
    left_rows = halves(left_ref[...].reshape(3 * W, W))
    stack = halves(jnp.concatenate([own_slot(mine, 0), own_slot(mine, 1)], axis=0))
    mixed[...] = split_product(stack, left_rows, 1).reshape(2, W, 3 * W)
    for i in range(2):
        present = [(1 - i + k, mixed_rows(mixed, k)) for k in range(2)]
        couple(own_row(table, i), present, moved_of(shifted, (), i)[1], None, True)


def early_part(mine, table, left_interface):
    vmem = pl.BlockSpec(memory_space=pltpu.VMEM)
    return pl.pallas_call(
        early_kernel,
        out_shape=pltpu.VMEM((3 * W, 2 * W), jnp.float32),
        in_specs=[vmem] * 3,
        out_specs=vmem,
        scratch_shapes=[pltpu.VMEM((2, W, 3 * W), jnp.float32)],
        compiler_params=pltpu.CompilerParams(vmem_limit_bytes=ROOM),
        name="early_part",
    )(*near(mine, table, left_interface))


def local_kernel(
    mine,
    low,
    high,
    ahead,
    behind,
    own_terms,
    table,
    shifted,
    left_ref,
    right_ref,
    blocks,
    owned,
    terms,
    mixed,
    coupled,
    moved,
    pair,
):
    weights = [own_row(table, 0), own_row(table, 1)]
    right_rows = halves(right_ref[...].reshape(3 * W, W))
    left_rows = halves(left_ref[...].reshape(3 * W, W))
    left_lanes = halves(jnp.concatenate([left_ref[0], left_ref[1], left_ref[2]], axis=1))
    contract(right_rows, [low[0:W], high[0:W]], terms, 0)
    places = [
        (sent_row(low), (2, term_rows(own_terms, 0))),
        (weights[0], (0, term_rows(terms, 0))),
        (weights[1], (2, term_rows(terms, 1))),
        (sent_row(high), (0, term_rows(own_terms, 1))),
    ]
    for i in range(4):
        couple(places[i][0], [places[i][1]], lanes_of(coupled, i)[1], None, False)
    applied = split_product(halves(coupled[...].reshape(4 * W, 3 * W)), left_lanes, 1)
    residual = [
        source[W : 2 * W] - applied[i * W : (i + 1) * W]
        for i, source in enumerate((low, behind, ahead, high))
    ]
    outer = [None, low[0:W], high[0:W]]
    pair[0], pair[3] = outer[1], outer[2]
    pair[1], pair[2] = own_slot(mine, 0), own_slot(mine, 1)
    for i in range(4):
        pair[4 + i] = residual[i]
    owned[0:W] = residual[1]
    owned[W : 2 * W] = residual[2]
    contract(right_rows, residual, terms, 0)
    along = jnp.zeros((1, 1), jnp.float32)
    energy = jnp.zeros((1, 1), jnp.float32)
    for i in range(2):
        present = [(offset, term_rows(terms, i + offset)) for offset in range(3)]
        couple(weights[i], present, lanes_of(coupled, i)[1], None, False)
    images = split_product(halves(coupled[0:2].reshape(2 * W, 3 * W)), left_lanes, 1)
    for i in range(2):
        image = images[i * W : (i + 1) * W]
        along = along + jnp.sum(pair[5 + i] * image, keepdims=True)
        energy = energy + jnp.sum(image * image, keepdims=True)

    stack = halves(jnp.concatenate([outer[1], outer[2]] + residual, axis=0))
    mixed[...] = split_product(stack, left_rows, 1).reshape(6, W, 3 * W)
    for i in range(2):
        base = moved_of(shifted, (), i)[0]
        present = [(2 * i, mixed_rows(mixed, i))]
        couple(weights[i], present, moved_of(moved, (0,), i)[1], base, True)
        present = [(offset, mixed_rows(mixed, 2 + i + offset)) for offset in range(3)]
        couple(weights[i], present, moved_of(moved, (1,), i)[1], None, True)

    both = jnp.concatenate(
        [
            jnp.concatenate([pair[1], pair[2]], axis=1),
            jnp.concatenate([pair[5], pair[6]], axis=1),
        ],
        axis=0,
    )
    split = halves(both)
    forms = [split_product(halves(moved[u]), split, 1) for u in range(2)]
    tables = [forms[0][:, :W], forms[0][:, W:] + forms[1][:, :W], forms[1][:, W:]]
    square = product_t(both, both)
    grams = [square[:W, :W], square[:W, W:] + square[W:, :W], square[W:, W:]]
    row, lane = iotas((HALF, W))
    for version in range(3):
        gram = grams[version]
        upper, under = gram[:HALF], gram[HALF:]
        for part in range(6):
            blocks[pl.ds(8 * version + part, HALF, stride=24), :] = tables[version][
                part * HALF : (part + 1) * HALF
            ]
        fold = jnp.where(lane <= row + HALF, under, pltpu.roll(upper, HALF, 1))
        blocks[pl.ds(8 * version + 6, HALF, stride=24), :] = fold
        diagonal = jnp.sum(jnp.where(lane == row, upper, 0.0), axis=1, keepdims=True)
        extra = jnp.where(lane == 0, diagonal, 0.0)
        if version == 0:
            extra = jnp.where(lane == 1, along, jnp.where(lane == 2, energy, extra))
        blocks[pl.ds(8 * version + 7, HALF, stride=24), :] = extra


def local_part(mine, low, high, ahead, behind, terms, table, shifted, left_interface, right_interface):
    vmem = pl.BlockSpec(memory_space=pltpu.VMEM)
    return pl.pallas_call(
        local_kernel,
        out_shape=(
            pltpu.VMEM((HALF * 24, W), jnp.float32),
            pltpu.VMEM((2 * W, W), jnp.float32),
        ),
        in_specs=[vmem] * 10,
        out_specs=(vmem, vmem),
        scratch_shapes=[
            pltpu.VMEM((4, 3 * W, W), jnp.float32),
            pltpu.VMEM((6, W, 3 * W), jnp.float32),
            pltpu.VMEM((4, W, 3 * W), jnp.float32),
            pltpu.VMEM((2, 3 * W, 2 * W), jnp.float32),
            pltpu.VMEM((8, W, W), jnp.float32),
        ],
        compiler_params=pltpu.CompilerParams(vmem_limit_bytes=ROOM),
        name="local_part",
    )(
        *near(
            mine,
            low,
            high,
            ahead,
            behind,
            terms,
            table,
            shifted,
            left_interface,
            right_interface,
        )
    )


def combine_kernel(got, out, alpha_ref, *, scale):
    count = got.shape[0] // 4
    parts = [jnp.sum(got[pl.ds(v, count, stride=4), :], axis=0, keepdims=True) for v in range(4)]
    lane = lax.broadcasted_iota(jnp.int32, (1, W), 1)
    along = jnp.sum(jnp.where(lane == 1, parts[3], 0.0), axis=1, keepdims=True)
    energy = jnp.sum(jnp.where(lane == 2, parts[3], 0.0), axis=1, keepdims=True)
    alpha = jnp.broadcast_to(along, (1, W)) / jnp.broadcast_to(energy, (1, W))
    alpha_ref[...] = jnp.broadcast_to(alpha, (8, W))
    block = (parts[0] + alpha * (parts[1] + alpha * parts[2])) * scale
    out[...] = jnp.broadcast_to(block, out.shape)


def combine_part(got, scale):
    vmem = pl.BlockSpec(memory_space=pltpu.VMEM)

    def kernel(*refs):
        combine_kernel(*refs, scale=scale)

    return pl.pallas_call(
        kernel,
        out_shape=(
            pltpu.VMEM((got.shape[0] // 4, W), jnp.float32),
            pltpu.VMEM((8, W), jnp.float32),
        ),
        in_specs=[vmem],
        out_specs=(vmem, vmem),
        compiler_params=pltpu.CompilerParams(vmem_limit_bytes=ROOM),
        name="combine_part",
    )(*near(got))


def factor_kernel(whole, alpha_ref, mine, owned, basis, triangle, inverse, table):
    row, lane = iotas((HALF, W))
    fold = whole[pl.ds(6, HALF, stride=8), :]
    extra = whole[pl.ds(7, HALF, stride=8), :]
    under = jnp.where(lane <= row + HALF, fold, 0.0)
    upper = jnp.where((lane > row) & (lane < HALF), pltpu.roll(fold, HALF, 1), 0.0)
    upper = upper + jnp.where(lane == row, jnp.broadcast_to(extra[:, :1], (HALF, W)), 0.0)
    zero = jnp.zeros((HALF, W), jnp.float32)
    lower_part = jnp.concatenate([zero, under], axis=0)
    upper_part = jnp.concatenate([upper, zero], axis=0)
    row, lane = iotas((W, W))
    lower_part = lower_part + jnp.where(lane < row, upper_part.T, 0.0)
    table[:, :W] = lower_part.T + jnp.where(lane < row, lower_part, 0.0) + upper_part - jnp.where(
        lane > row, upper_part, 0.0
    )
    table[:, W:] = jnp.where(lane == row, 1.0, 0.0)

    sub, across = iotas((SIZE, W))
    for first in range(0, W, SIZE):
        last = first + SIZE
        panel = table[first:last, :]
        left, right = panel[:, :W], panel[:, W:]
        columns = [
            jnp.broadcast_to(left[:, first + k : first + k + 1], (SIZE, W)) for k in range(SIZE)
        ]
        for k in range(SIZE):
            pivot = jnp.broadcast_to(columns[k][k : k + 1, :], (SIZE, W))
            root = lax.rsqrt(pivot)
            root = root * (1.5 - 0.5 * pivot * (root * root))
            factor = jnp.where(sub > k, columns[k] * (root * root), 0.0)

            def spread(value):
                return jnp.broadcast_to(value[k : k + 1, :], (SIZE, W))

            for j in range(k + 1, SIZE):
                columns[j] = columns[j] - factor * spread(columns[j])
            head = spread(left)
            left = jnp.where(sub == k, head * root, left - factor * head)
            head = spread(right)
            right = jnp.where(sub == k, head * root, right - factor * head)
        left = jnp.where(across >= sub + first, left, 0.0)
        triangle[first:last, :] = left
        inverse[first:last, :] = right
        if last < W:
            done = jnp.concatenate([left, right], axis=1)
            turned = left.T
            for low, high in ((last, last + SIZE), (last + SIZE, W)):
                if low < high:
                    table[low:high, :] = table[low:high, :] - product(turned[low:high], done)

    alpha = alpha_ref[0:1, :]
    core = [
        mine[:, i].reshape(W, W) + alpha * owned[i * W : (i + 1) * W] for i in range(2)
    ]
    both = product(inverse[...], jnp.concatenate(core, axis=1))
    for i in range(2):
        basis[:, i] = both[:, i * W : (i + 1) * W].reshape(basis.shape[0], basis.shape[2], W)


def interface_kernel(rank, whole, inverse, out):
    rows = out.shape[1]
    start = pl.multiple_of(rank[0] * rows, rows)
    mine = inverse[pl.ds(start, rows), :]
    parts = []
    for beta in range(3):
        halves = [whole[pl.ds(2 * beta + h, HALF, stride=8), :] for h in range(2)]
        parts.append(product(mine, jnp.concatenate(halves, axis=0)))
    result = product_t(jnp.concatenate(parts, axis=0), inverse[...])
    out[...] = result.reshape(3, rows, W)


def final_part(whole, alpha, mine, owned, rank):
    vmem = pl.BlockSpec(memory_space=pltpu.VMEM)
    ranks, _, piece, _ = mine.shape
    basis, triangle, inverse = pl.pallas_call(
        factor_kernel,
        out_shape=(
            pltpu.VMEM((ranks, 2, piece, W), jnp.float32),
            jax.ShapeDtypeStruct((W, W), jnp.float32),
            pltpu.VMEM((W, W), jnp.float32),
        ),
        in_specs=[vmem] * 4,
        out_specs=(vmem,) * 3,
        scratch_shapes=[pltpu.VMEM((W, 2 * W), jnp.float32)],
        compiler_params=pltpu.CompilerParams(vmem_limit_bytes=ROOM),
        name="factor_part",
    )(*near(whole, alpha, mine, owned))
    interface = pl.pallas_call(
        interface_kernel,
        out_shape=jax.ShapeDtypeStruct((3, piece, W), jnp.float32),
        in_specs=[pl.BlockSpec(memory_space=pltpu.SMEM), vmem, vmem],
        out_specs=vmem,
        compiler_params=pltpu.CompilerParams(vmem_limit_bytes=ROOM),
        name="interface_part",
    )(rank, *near(whole, inverse))
    return basis, triangle, interface


def shards(start_core, right_side, left_interface, right_interface, couplings):
    height, piece, width = start_core.shape
    ranks = lax.axis_size("rank")
    slabs = lax.axis_size(("x", "y", "core"))
    count = slabs * ranks
    own = height // ranks
    assert width == W and own == 2 and slabs == HALF
    rank_index = lax.axis_index("rank")
    scale = 1.0 / (height * slabs * width)

    start = start_core.reshape(ranks, own, piece, width)
    right = right_side.reshape(ranks, own, piece, width)
    mine = exchange(pack_part(start, right), "rank")

    table = lax.dynamic_slice_in_dim(couplings.reshape(27, height), rank_index * own, own, 1)
    table = jnp.pad(table, ((0, 5), (0, 0))).T[:, :, None]
    table = jnp.broadcast_to(table, (own, 32, width)).reshape(own * 32, width)
    forward = [(i, i + 1) for i in range(count - 1)]
    backward = [(target, source) for source, target in forward]

    ahead, behind, terms = parcel_part(mine, table, left_interface, right_interface)
    low = lax.ppermute(ahead, ("x", "y", "core", "rank"), forward)
    high = lax.ppermute(behind, ("x", "y", "core", "rank"), backward)
    shifted = early_part(mine, table, left_interface)
    blocks, owned = local_part(
        mine, low, high, ahead, behind, terms, table, shifted, left_interface, right_interface
    )

    block = jnp.sum(exchange(blocks.reshape(8, 192, width), ("x", "core")), axis=0)
    block = block.reshape(8, 3, 8, width)
    sums = jnp.broadcast_to(block[:1, :1, 7:, :], (8, 8, 1, width))
    block = jnp.concatenate([block.transpose(0, 2, 1, 3), sums], axis=2)
    block = exchange(block.reshape(64, 4, width), ("y", "rank")).reshape(256, width)
    block, alpha = combine_part(block, scale)
    block = exchange(block.reshape(64, 1, width), ("y", "rank")).reshape(64, width)
    whole = exchange(jnp.broadcast_to(block, (8, 64, width)), ("x", "core"))

    rank = jnp.full((1,), rank_index, jnp.int32)
    basis, triangle, interface = final_part(whole.reshape(512, width), alpha, mine, owned, rank)
    output = exchange(basis, "rank").reshape(height, piece, width)
    return (output, triangle, interface)


def solution(mesh):
    names = ("x", "y", "core")
    fine = Mesh(mesh.devices.reshape(4, 8, 2, 8), names + ("rank",))
    placed = (P(names, "rank", None), P(names, "rank", None), P(), P(), P(None, None, None, names))
    return jax.shard_map(
        shards,
        mesh=fine,
        in_specs=placed,
        out_specs=(P(names, "rank", None), P(), P(None, "rank", None)),
        check_vma=False,
    )
```

```python
import jax
import jax.numpy as jnp
from jax import lax
from jax.experimental import pallas as pl
from jax.experimental.pallas import tpu as pltpu
from jax.sharding import Mesh
from jax.sharding import PartitionSpec as P

highest = lax.Precision.HIGHEST
W = 128
HALF = W // 2
SIZE = 16
ROOM = 16 * 2**20


def exchange(blocks, axis):
    return lax.all_to_all(blocks, axis, 0, 0, tiled=True)


def product(left, right):
    return jnp.dot(left, right, precision=highest, preferred_element_type=jnp.float32)


def product_t(left, right):
    return lax.dot_general(
        left,
        right,
        (((1,), (1,)), ((), ())),
        precision=highest,
        preferred_element_type=jnp.float32,
    )


def halves(value):
    high = value.astype(jnp.bfloat16)
    return high, (value - high.astype(jnp.float32)).astype(jnp.bfloat16)


def split_product(left, right, contract):
    def one(a, b):
        return lax.dot_general(
            a, b, (((1,), (contract,)), ((), ())), preferred_element_type=jnp.float32
        )

    return one(left[0], right[0]) + (one(left[0], right[1]) + one(left[1], right[0]))


def iotas(shape):
    return lax.broadcasted_iota(jnp.int32, shape, 0), lax.broadcasted_iota(jnp.int32, shape, 1)


def near(*values):
    return [pltpu.with_memory_space_constraint(value, pltpu.VMEM) for value in values]


def own_slot(mine, index):
    return mine[:, index].reshape(W, W)


def contract(right_rows, values, terms, first):
    for k in range(0, len(values), 2):
        both = split_product(right_rows, halves(jnp.concatenate(values[k : k + 2], axis=1)), 0)
        terms[first + k] = both[:, :W]
        terms[first + k + 1] = both[:, W:]


def couple(place, sources, target, base, left_first):
    used = {offset for offset, _ in sources}
    weight = {
        (i, j, offset): jnp.broadcast_to(place(i, j, offset), (8, W))
        for i in range(3)
        for j in range(3)
        for offset in used
    }

    def step(chunk, carry):
        at = pl.multiple_of(chunk * 8, 8)
        sums = [None if base is None else base(index, at) for index in range(3)]
        for offset, rows in sources:
            for inner in range(3):
                value = rows(inner, at)
                for outer in range(3):
                    key = (inner, outer) if left_first else (outer, inner)
                    part = weight[key + (offset,)] * value
                    sums[outer] = part if sums[outer] is None else sums[outer] + part
        for index in range(3):
            target(index, at, sums[index])
        return carry

    lax.fori_loop(0, W // 8, step, 0, unroll=2)


def term_rows(terms, place):
    return lambda index, at: terms[place, pl.ds(index * W + at, 8), :]


def mixed_rows(mixed, place):
    return lambda index, at: mixed[place, pl.ds(at, 8), index * W : (index + 1) * W]


def lanes_of(ref, place):
    def load(index, at):
        return ref[place, pl.ds(at, 8), index * W : (index + 1) * W]

    def store(index, at, value):
        ref[place, pl.ds(at, 8), index * W : (index + 1) * W] = value

    return load, store


def moved_of(ref, lead, place):
    def load(index, at):
        return ref[lead + (pl.ds(index * W + at, 8), slice(place * W, (place + 1) * W))]

    def store(index, at, value):
        ref[lead + (pl.ds(index * W + at, 8), slice(place * W, (place + 1) * W))] = value

    return load, store


def own_row(table, mode):
    def row(i, j, offset):
        at = 32 * mode + 9 * i + 3 * j + offset
        return table[at : at + 1, :]

    return row


def sent_row(parcel):
    return lambda i, j, offset: parcel[2 * W + 3 * i + j : 2 * W + 3 * i + j + 1, :]


def parcel_kernel(mine, table, left_ref, right_ref, ahead, behind, terms, coupled):
    right_rows = halves(right_ref[...].reshape(3 * W, W))
    left_lanes = halves(jnp.concatenate([left_ref[0], left_ref[1], left_ref[2]], axis=1))
    contract(right_rows, [own_slot(mine, 0), own_slot(mine, 1)], terms, 0)
    for i in range(2):
        present = [(1 - i + k, term_rows(terms, k)) for k in range(2)]
        couple(own_row(table, i), present, lanes_of(coupled, i)[1], None, False)
    applied = split_product(halves(coupled[...].reshape(2 * W, 3 * W)), left_lanes, 1)
    for i, parcel, offset in ((0, behind, 0), (1, ahead, 2)):
        parcel[0:W] = own_slot(mine, i)
        parcel[W : 2 * W] = own_slot(mine, 2 + i) - applied[i * W : (i + 1) * W]
        parcel[2 * W : 2 * W + 16] = jnp.zeros((16, W), jnp.float32)
        row = own_row(table, i)
        for alpha in range(3):
            for beta in range(3):
                at = 2 * W + 3 * alpha + beta
                parcel[at : at + 1, :] = row(alpha, beta, offset)


def parcel_part(mine, table, left_interface, right_interface):
    vmem = pl.BlockSpec(memory_space=pltpu.VMEM)
    return pl.pallas_call(
        parcel_kernel,
        out_shape=(
            pltpu.VMEM((2 * W + 16, W), jnp.float32),
            pltpu.VMEM((2 * W + 16, W), jnp.float32),
            pltpu.VMEM((2, 3 * W, W), jnp.float32),
        ),
        in_specs=[vmem] * 4,
        out_specs=(vmem,) * 3,
        scratch_shapes=[pltpu.VMEM((2, W, 3 * W), jnp.float32)],
        compiler_params=pltpu.CompilerParams(vmem_limit_bytes=ROOM),
        name="parcel_part",
    )(*near(mine, table, left_interface, right_interface))


def early_kernel(mine, table, left_ref, shifted, mixed):
    left_rows = halves(left_ref[...].reshape(3 * W, W))
    stack = halves(jnp.concatenate([own_slot(mine, 0), own_slot(mine, 1)], axis=0))
    mixed[...] = split_product(stack, left_rows, 1).reshape(2, W, 3 * W)
    for i in range(2):
        present = [(1 - i + k, mixed_rows(mixed, k)) for k in range(2)]
        couple(own_row(table, i), present, moved_of(shifted, (), i)[1], None, True)


def early_part(mine, table, left_interface):
    vmem = pl.BlockSpec(memory_space=pltpu.VMEM)
    return pl.pallas_call(
        early_kernel,
        out_shape=pltpu.VMEM((3 * W, 2 * W), jnp.float32),
        in_specs=[vmem] * 3,
        out_specs=vmem,
        scratch_shapes=[pltpu.VMEM((2, W, 3 * W), jnp.float32)],
        compiler_params=pltpu.CompilerParams(vmem_limit_bytes=ROOM),
        name="early_part",
    )(*near(mine, table, left_interface))


def local_kernel(
    mine,
    low,
    high,
    ahead,
    behind,
    own_terms,
    table,
    shifted,
    left_ref,
    right_ref,
    blocks,
    owned,
    terms,
    mixed,
    coupled,
    moved,
    pair,
):
    weights = [own_row(table, 0), own_row(table, 1)]
    right_rows = halves(right_ref[...].reshape(3 * W, W))
    left_rows = halves(left_ref[...].reshape(3 * W, W))
    left_lanes = halves(jnp.concatenate([left_ref[0], left_ref[1], left_ref[2]], axis=1))
    contract(right_rows, [low[0:W], high[0:W]], terms, 0)
    places = [
        (sent_row(low), (2, term_rows(own_terms, 0))),
        (weights[0], (0, term_rows(terms, 0))),
        (weights[1], (2, term_rows(terms, 1))),
        (sent_row(high), (0, term_rows(own_terms, 1))),
    ]
    for i in range(4):
        couple(places[i][0], [places[i][1]], lanes_of(coupled, i)[1], None, False)
    applied = split_product(halves(coupled[...].reshape(4 * W, 3 * W)), left_lanes, 1)
    residual = [
        source[W : 2 * W] - applied[i * W : (i + 1) * W]
        for i, source in enumerate((low, behind, ahead, high))
    ]
    outer = [None, low[0:W], high[0:W]]
    pair[0], pair[3] = outer[1], outer[2]
    pair[1], pair[2] = own_slot(mine, 0), own_slot(mine, 1)
    for i in range(4):
        pair[4 + i] = residual[i]
    owned[0:W] = residual[1]
    owned[W : 2 * W] = residual[2]
    contract(right_rows, residual, terms, 0)
    along = jnp.zeros((1, 1), jnp.float32)
    energy = jnp.zeros((1, 1), jnp.float32)
    for i in range(2):
        present = [(offset, term_rows(terms, i + offset)) for offset in range(3)]
        couple(weights[i], present, lanes_of(coupled, i)[1], None, False)
    images = split_product(halves(coupled[0:2].reshape(2 * W, 3 * W)), left_lanes, 1)
    for i in range(2):
        image = images[i * W : (i + 1) * W]
        along = along + jnp.sum(pair[5 + i] * image, keepdims=True)
        energy = energy + jnp.sum(image * image, keepdims=True)

    stack = halves(jnp.concatenate([outer[1], outer[2]] + residual, axis=0))
    mixed[...] = split_product(stack, left_rows, 1).reshape(6, W, 3 * W)
    for i in range(2):
        base = moved_of(shifted, (), i)[0]
        present = [(2 * i, mixed_rows(mixed, i))]
        couple(weights[i], present, moved_of(moved, (0,), i)[1], base, True)
        present = [(offset, mixed_rows(mixed, 2 + i + offset)) for offset in range(3)]
        couple(weights[i], present, moved_of(moved, (1,), i)[1], None, True)

    both = jnp.concatenate(
        [
            jnp.concatenate([pair[1], pair[2]], axis=1),
            jnp.concatenate([pair[5], pair[6]], axis=1),
        ],
        axis=0,
    )
    split = halves(both)
    forms = [split_product(halves(moved[u]), split, 1) for u in range(2)]
    tables = [forms[0][:, :W], forms[0][:, W:] + forms[1][:, :W], forms[1][:, W:]]
    square = product_t(both, both)
    grams = [square[:W, :W], square[:W, W:] + square[W:, :W], square[W:, W:]]
    row, lane = iotas((HALF, W))
    for version in range(3):
        gram = grams[version]
        upper, under = gram[:HALF], gram[HALF:]
        for part in range(6):
            blocks[pl.ds(8 * version + part, HALF, stride=24), :] = tables[version][
                part * HALF : (part + 1) * HALF
            ]
        fold = jnp.where(lane <= row + HALF, under, pltpu.roll(upper, HALF, 1))
        blocks[pl.ds(8 * version + 6, HALF, stride=24), :] = fold
        diagonal = jnp.sum(jnp.where(lane == row, upper, 0.0), axis=1, keepdims=True)
        extra = jnp.where(lane == 0, diagonal, 0.0)
        if version == 0:
            extra = jnp.where(lane == 1, along, jnp.where(lane == 2, energy, extra))
        blocks[pl.ds(8 * version + 7, HALF, stride=24), :] = extra


def local_part(mine, low, high, ahead, behind, terms, table, shifted, left_interface, right_interface):
    vmem = pl.BlockSpec(memory_space=pltpu.VMEM)
    return pl.pallas_call(
        local_kernel,
        out_shape=(
            pltpu.VMEM((HALF * 24, W), jnp.float32),
            pltpu.VMEM((2 * W, W), jnp.float32),
        ),
        in_specs=[vmem] * 10,
        out_specs=(vmem, vmem),
        scratch_shapes=[
            pltpu.VMEM((4, 3 * W, W), jnp.float32),
            pltpu.VMEM((6, W, 3 * W), jnp.float32),
            pltpu.VMEM((4, W, 3 * W), jnp.float32),
            pltpu.VMEM((2, 3 * W, 2 * W), jnp.float32),
            pltpu.VMEM((8, W, W), jnp.float32),
        ],
        compiler_params=pltpu.CompilerParams(vmem_limit_bytes=ROOM),
        name="local_part",
    )(
        *near(
            mine,
            low,
            high,
            ahead,
            behind,
            terms,
            table,
            shifted,
            left_interface,
            right_interface,
        )
    )


def combine_kernel(got, out, alpha_ref, *, scale):
    count = got.shape[0] // 4
    parts = [jnp.sum(got[pl.ds(v, count, stride=4), :], axis=0, keepdims=True) for v in range(4)]
    lane = lax.broadcasted_iota(jnp.int32, (1, W), 1)
    along = jnp.sum(jnp.where(lane == 1, parts[3], 0.0), axis=1, keepdims=True)
    energy = jnp.sum(jnp.where(lane == 2, parts[3], 0.0), axis=1, keepdims=True)
    alpha = jnp.broadcast_to(along, (1, W)) / jnp.broadcast_to(energy, (1, W))
    alpha_ref[...] = jnp.broadcast_to(alpha, (8, W))
    block = (parts[0] + alpha * (parts[1] + alpha * parts[2])) * scale
    out[...] = jnp.broadcast_to(block, out.shape)


def combine_part(got, scale):
    vmem = pl.BlockSpec(memory_space=pltpu.VMEM)

    def kernel(*refs):
        combine_kernel(*refs, scale=scale)

    return pl.pallas_call(
        kernel,
        out_shape=(
            pltpu.VMEM((got.shape[0] // 4, W), jnp.float32),
            pltpu.VMEM((8, W), jnp.float32),
        ),
        in_specs=[vmem],
        out_specs=(vmem, vmem),
        compiler_params=pltpu.CompilerParams(vmem_limit_bytes=ROOM),
        name="combine_part",
    )(*near(got))


def factor_kernel(whole, alpha_ref, mine, owned, basis, triangle, inverse, table):
    row, lane = iotas((HALF, W))
    fold = whole[pl.ds(6, HALF, stride=8), :]
    extra = whole[pl.ds(7, HALF, stride=8), :]
    under = jnp.where(lane <= row + HALF, fold, 0.0)
    upper = jnp.where((lane > row) & (lane < HALF), pltpu.roll(fold, HALF, 1), 0.0)
    upper = upper + jnp.where(lane == row, jnp.broadcast_to(extra[:, :1], (HALF, W)), 0.0)
    zero = jnp.zeros((HALF, W), jnp.float32)
    lower_part = jnp.concatenate([zero, under], axis=0)
    upper_part = jnp.concatenate([upper, zero], axis=0)
    row, lane = iotas((W, W))
    lower_part = lower_part + jnp.where(lane < row, upper_part.T, 0.0)
    table[:, :W] = lower_part.T + jnp.where(lane < row, lower_part, 0.0) + upper_part - jnp.where(
        lane > row, upper_part, 0.0
    )
    table[:, W:] = jnp.where(lane == row, 1.0, 0.0)

    sub, across = iotas((SIZE, W))
    for first in range(0, W, SIZE):
        last = first + SIZE
        panel = table[first:last, :]
        left, right = panel[:, :W], panel[:, W:]
        columns = [
            jnp.broadcast_to(left[:, first + k : first + k + 1], (SIZE, W)) for k in range(SIZE)
        ]
        for k in range(SIZE):
            pivot = jnp.broadcast_to(columns[k][k : k + 1, :], (SIZE, W))
            root = lax.rsqrt(pivot)
            root = root * (1.5 - 0.5 * pivot * (root * root))
            factor = jnp.where(sub > k, columns[k] * (root * root), 0.0)

            def spread(value):
                return jnp.broadcast_to(value[k : k + 1, :], (SIZE, W))

            for j in range(k + 1, SIZE):
                columns[j] = columns[j] - factor * spread(columns[j])
            head = spread(left)
            left = jnp.where(sub == k, head * root, left - factor * head)
            head = spread(right)
            right = jnp.where(sub == k, head * root, right - factor * head)
        left = jnp.where(across >= sub + first, left, 0.0)
        triangle[first:last, :] = left
        inverse[first:last, :] = right
        if last < W:
            done = jnp.concatenate([left, right], axis=1)
            turned = left.T
            for low, high in ((last, last + SIZE), (last + SIZE, W)):
                if low < high:
                    table[low:high, :] = table[low:high, :] - product(turned[low:high], done)

    alpha = alpha_ref[0:1, :]
    core = [
        mine[:, i].reshape(W, W) + alpha * owned[i * W : (i + 1) * W] for i in range(2)
    ]
    both = product(inverse[...], jnp.concatenate(core, axis=1))
    for i in range(2):
        basis[:, i] = both[:, i * W : (i + 1) * W].reshape(basis.shape[0], basis.shape[2], W)


def interface_kernel(rank, whole, inverse, out):
    rows = out.shape[1]
    start = pl.multiple_of(rank[0] * rows, rows)
    mine = inverse[pl.ds(start, rows), :]
    parts = []
    for beta in range(3):
        halves = [whole[pl.ds(2 * beta + h, HALF, stride=8), :] for h in range(2)]
        parts.append(product(mine, jnp.concatenate(halves, axis=0)))
    result = product_t(jnp.concatenate(parts, axis=0), inverse[...])
    out[...] = result.reshape(3, rows, W)


def final_part(whole, alpha, mine, owned, rank):
    vmem = pl.BlockSpec(memory_space=pltpu.VMEM)
    ranks, _, piece, _ = mine.shape
    basis, triangle, inverse = pl.pallas_call(
        factor_kernel,
        out_shape=(
            pltpu.VMEM((ranks, 2, piece, W), jnp.float32),
            jax.ShapeDtypeStruct((W, W), jnp.float32),
            pltpu.VMEM((W, W), jnp.float32),
        ),
        in_specs=[vmem] * 4,
        out_specs=(vmem,) * 3,
        scratch_shapes=[pltpu.VMEM((W, 2 * W), jnp.float32)],
        compiler_params=pltpu.CompilerParams(vmem_limit_bytes=ROOM),
        name="factor_part",
    )(*near(whole, alpha, mine, owned))
    interface = pl.pallas_call(
        interface_kernel,
        out_shape=jax.ShapeDtypeStruct((3, piece, W), jnp.float32),
        in_specs=[pl.BlockSpec(memory_space=pltpu.SMEM), vmem, vmem],
        out_specs=vmem,
        compiler_params=pltpu.CompilerParams(vmem_limit_bytes=ROOM),
        name="interface_part",
    )(rank, *near(whole, inverse))
    return basis, triangle, interface


def shards(start_core, right_side, left_interface, right_interface, couplings):
    height, piece, width = start_core.shape
    ranks = lax.axis_size("rank")
    slabs = lax.axis_size(("x", "y", "core"))
    count = slabs * ranks
    own = height // ranks
    assert width == W and own == 2 and slabs == HALF
    rank_index = lax.axis_index("rank")
    scale = 1.0 / (height * slabs * width)

    start = start_core.reshape(ranks, own, piece, width)
    right = right_side.reshape(ranks, own, piece, width)
    odd = lax.axis_index("core") == 1
    packed = jnp.concatenate([start, right], axis=1)
    mine = exchange(jnp.where(odd, packed[::-1], packed), "rank")

    chunk = jnp.where(odd, ranks - 1 - rank_index, rank_index)
    table = lax.dynamic_slice_in_dim(couplings.reshape(27, height), chunk * own, own, 1)
    table = jnp.pad(table, ((0, 5), (0, 0))).T[:, :, None]
    table = jnp.broadcast_to(table, (own, 32, width)).reshape(own * 32, width)
    order = [
        slab * ranks + (part if slab % 2 == 0 else ranks - 1 - part)
        for slab in range(slabs)
        for part in range(ranks)
    ]
    forward = list(zip(order[:-1], order[1:]))
    backward = [(target, source) for source, target in forward]

    ahead, behind, terms = parcel_part(mine, table, left_interface, right_interface)
    low = lax.ppermute(ahead, ("x", "y", "core", "rank"), forward)
    high = lax.ppermute(behind, ("x", "y", "core", "rank"), backward)
    shifted = early_part(mine, table, left_interface)
    blocks, owned = local_part(
        mine, low, high, ahead, behind, terms, table, shifted, left_interface, right_interface
    )

    block = jnp.sum(exchange(blocks.reshape(8, 192, width), ("x", "core")), axis=0)
    block = block.reshape(8, 3, 8, width)
    sums = jnp.broadcast_to(block[:1, :1, 7:, :], (8, 8, 1, width))
    block = jnp.concatenate([block.transpose(0, 2, 1, 3), sums], axis=2)
    block = exchange(block.reshape(64, 4, width), ("y", "rank")).reshape(256, width)
    block, alpha = combine_part(block, scale)
    block = exchange(block.reshape(64, 1, width), ("y", "rank")).reshape(64, width)
    whole = exchange(jnp.broadcast_to(block, (8, 64, width)), ("x", "core"))

    rank = jnp.full((1,), rank_index, jnp.int32)
    basis, triangle, interface = final_part(whole.reshape(512, width), alpha, mine, owned, rank)
    output = exchange(basis, "rank")
    output = jnp.where(odd, output[::-1], output).reshape(height, piece, width)
    return (output, triangle, interface)


def solution(mesh):
    names = ("x", "y", "core")
    fine = Mesh(mesh.devices.reshape(4, 8, 2, 8), names + ("rank",))
    placed = (P(names, "rank", None), P(names, "rank", None), P(), P(), P(None, None, None, names))
    return jax.shard_map(
        shards,
        mesh=fine,
        in_specs=placed,
        out_specs=(P(names, "rank", None), P(), P(None, "rank", None)),
        check_vma=False,
    )
```

```python
import jax
import jax.numpy as jnp
from jax import lax
from jax.experimental import pallas as pl
from jax.experimental.pallas import tpu as pltpu
from jax.sharding import Mesh
from jax.sharding import PartitionSpec as P

highest = lax.Precision.HIGHEST
W = 128
HALF = W // 2
SIZE = 16
ROOM = 16 * 2**20


def exchange(blocks, axis):
    return lax.all_to_all(blocks, axis, 0, 0, tiled=True)


def product(left, right):
    return jnp.dot(left, right, precision=highest, preferred_element_type=jnp.float32)


def product_t(left, right):
    return lax.dot_general(
        left,
        right,
        (((1,), (1,)), ((), ())),
        precision=highest,
        preferred_element_type=jnp.float32,
    )


def halves(value):
    high = value.astype(jnp.bfloat16)
    return high, (value - high.astype(jnp.float32)).astype(jnp.bfloat16)


def split_product(left, right, contract):
    def one(a, b):
        return lax.dot_general(
            a, b, (((1,), (contract,)), ((), ())), preferred_element_type=jnp.float32
        )

    return one(left[0], right[0]) + (one(left[0], right[1]) + one(left[1], right[0]))


def iotas(shape):
    return lax.broadcasted_iota(jnp.int32, shape, 0), lax.broadcasted_iota(jnp.int32, shape, 1)


def near(*values):
    return [pltpu.with_memory_space_constraint(value, pltpu.VMEM) for value in values]


def part_of(whole, part):
    return jnp.concatenate([whole[64 * y + 8 * part : 64 * y + 8 * part + 8] for y in range(8)])


def own_slot(mine, index):
    return mine[:, index].reshape(W, W)


def contract(right_rows, values, terms, first):
    for k in range(0, len(values), 2):
        both = split_product(right_rows, halves(jnp.concatenate(values[k : k + 2], axis=1)), 0)
        terms[first + k] = both[:, :W]
        terms[first + k + 1] = both[:, W:]


def couple(place, sources, target, base, left_first):
    used = {offset for offset, _ in sources}
    weight = {
        (i, j, offset): jnp.broadcast_to(place(i, j, offset), (8, W))
        for i in range(3)
        for j in range(3)
        for offset in used
    }

    def step(chunk, carry):
        at = pl.multiple_of(chunk * 8, 8)
        sums = [None if base is None else base(index, at) for index in range(3)]
        for offset, rows in sources:
            for inner in range(3):
                value = rows(inner, at)
                for outer in range(3):
                    key = (inner, outer) if left_first else (outer, inner)
                    part = weight[key + (offset,)] * value
                    sums[outer] = part if sums[outer] is None else sums[outer] + part
        for index in range(3):
            target(index, at, sums[index])
        return carry

    lax.fori_loop(0, W // 8, step, 0, unroll=2)


def term_rows(terms, place):
    return lambda index, at: terms[place, pl.ds(index * W + at, 8), :]


def mixed_rows(mixed, place):
    return lambda index, at: mixed[place, pl.ds(at, 8), index * W : (index + 1) * W]


def lanes_of(ref, place):
    def load(index, at):
        return ref[place, pl.ds(at, 8), index * W : (index + 1) * W]

    def store(index, at, value):
        ref[place, pl.ds(at, 8), index * W : (index + 1) * W] = value

    return load, store


def moved_of(ref, lead, place):
    def load(index, at):
        return ref[lead + (pl.ds(index * W + at, 8), slice(place * W, (place + 1) * W))]

    def store(index, at, value):
        ref[lead + (pl.ds(index * W + at, 8), slice(place * W, (place + 1) * W))] = value

    return load, store


def own_row(table, mode):
    def row(i, j, offset):
        at = 32 * mode + 9 * i + 3 * j + offset
        return table[at : at + 1, :]

    return row


def sent_row(parcel):
    return lambda i, j, offset: parcel[2 * W + 3 * i + j : 2 * W + 3 * i + j + 1, :]


def parcel_kernel(mine, table, left_ref, right_ref, ahead, behind, terms, coupled):
    right_rows = halves(right_ref[...].reshape(3 * W, W))
    left_lanes = halves(jnp.concatenate([left_ref[0], left_ref[1], left_ref[2]], axis=1))
    contract(right_rows, [own_slot(mine, 0), own_slot(mine, 1)], terms, 0)
    for i in range(2):
        present = [(1 - i + k, term_rows(terms, k)) for k in range(2)]
        couple(own_row(table, i), present, lanes_of(coupled, i)[1], None, False)
    applied = split_product(halves(coupled[...].reshape(2 * W, 3 * W)), left_lanes, 1)
    for i, parcel, offset in ((0, behind, 0), (1, ahead, 2)):
        parcel[0:W] = own_slot(mine, i)
        parcel[W : 2 * W] = own_slot(mine, 2 + i) - applied[i * W : (i + 1) * W]
        parcel[2 * W : 2 * W + 16] = jnp.zeros((16, W), jnp.float32)
        row = own_row(table, i)
        for alpha in range(3):
            for beta in range(3):
                at = 2 * W + 3 * alpha + beta
                parcel[at : at + 1, :] = row(alpha, beta, offset)


def parcel_part(mine, table, left_interface, right_interface):
    vmem = pl.BlockSpec(memory_space=pltpu.VMEM)
    return pl.pallas_call(
        parcel_kernel,
        out_shape=(
            pltpu.VMEM((2 * W + 16, W), jnp.float32),
            pltpu.VMEM((2 * W + 16, W), jnp.float32),
            pltpu.VMEM((2, 3 * W, W), jnp.float32),
        ),
        in_specs=[vmem] * 4,
        out_specs=(vmem,) * 3,
        scratch_shapes=[pltpu.VMEM((2, W, 3 * W), jnp.float32)],
        compiler_params=pltpu.CompilerParams(vmem_limit_bytes=ROOM),
        name="parcel_part",
    )(*near(mine, table, left_interface, right_interface))


def early_kernel(mine, table, left_ref, shifted, square, mixed):
    left_rows = halves(left_ref[...].reshape(3 * W, W))
    stack = halves(jnp.concatenate([own_slot(mine, 0), own_slot(mine, 1)], axis=0))
    mixed[...] = split_product(stack, left_rows, 1).reshape(2, W, 3 * W)
    wide = jnp.concatenate([own_slot(mine, 0), own_slot(mine, 1)], axis=1)
    square[...] = product_t(wide, wide)
    for i in range(2):
        present = [(1 - i + k, mixed_rows(mixed, k)) for k in range(2)]
        couple(own_row(table, i), present, moved_of(shifted, (), i)[1], None, True)


def early_part(mine, table, left_interface):
    vmem = pl.BlockSpec(memory_space=pltpu.VMEM)
    return pl.pallas_call(
        early_kernel,
        out_shape=(
            pltpu.VMEM((3 * W, 2 * W), jnp.float32),
            pltpu.VMEM((W, W), jnp.float32),
        ),
        in_specs=[vmem] * 3,
        out_specs=(vmem, vmem),
        scratch_shapes=[pltpu.VMEM((2, W, 3 * W), jnp.float32)],
        compiler_params=pltpu.CompilerParams(vmem_limit_bytes=ROOM),
        name="early_part",
    )(*near(mine, table, left_interface))


def local_kernel(
    mine,
    low,
    high,
    ahead,
    behind,
    own_terms,
    table,
    shifted,
    start_gram,
    left_ref,
    right_ref,
    blocks,
    owned,
    terms,
    mixed,
    coupled,
    moved,
    pair,
):
    weights = [own_row(table, 0), own_row(table, 1)]
    right_rows = halves(right_ref[...].reshape(3 * W, W))
    left_rows = halves(left_ref[...].reshape(3 * W, W))
    left_lanes = halves(jnp.concatenate([left_ref[0], left_ref[1], left_ref[2]], axis=1))
    contract(right_rows, [low[0:W], high[0:W]], terms, 0)
    places = [
        (sent_row(low), (2, term_rows(own_terms, 0))),
        (weights[0], (0, term_rows(terms, 0))),
        (weights[1], (2, term_rows(terms, 1))),
        (sent_row(high), (0, term_rows(own_terms, 1))),
    ]
    for i in range(4):
        couple(places[i][0], [places[i][1]], lanes_of(coupled, i)[1], None, False)
    applied = split_product(halves(coupled[...].reshape(4 * W, 3 * W)), left_lanes, 1)
    residual = [
        source[W : 2 * W] - applied[i * W : (i + 1) * W]
        for i, source in enumerate((low, behind, ahead, high))
    ]
    outer = [None, low[0:W], high[0:W]]
    pair[0], pair[3] = outer[1], outer[2]
    pair[1], pair[2] = own_slot(mine, 0), own_slot(mine, 1)
    for i in range(4):
        pair[4 + i] = residual[i]
    owned[0:W] = residual[1]
    owned[W : 2 * W] = residual[2]
    contract(right_rows, residual, terms, 0)
    along = jnp.zeros((1, 1), jnp.float32)
    energy = jnp.zeros((1, 1), jnp.float32)
    for i in range(2):
        present = [(offset, term_rows(terms, i + offset)) for offset in range(3)]
        couple(weights[i], present, lanes_of(coupled, i)[1], None, False)
    images = split_product(halves(coupled[0:2].reshape(2 * W, 3 * W)), left_lanes, 1)
    for i in range(2):
        image = images[i * W : (i + 1) * W]
        along = along + jnp.sum(pair[5 + i] * image, keepdims=True)
        energy = energy + jnp.sum(image * image, keepdims=True)

    stack = halves(jnp.concatenate([outer[1], outer[2]] + residual, axis=0))
    mixed[...] = split_product(stack, left_rows, 1).reshape(6, W, 3 * W)
    for i in range(2):
        base = moved_of(shifted, (), i)[0]
        present = [(2 * i, mixed_rows(mixed, i))]
        couple(weights[i], present, moved_of(moved, (0,), i)[1], base, True)
        present = [(offset, mixed_rows(mixed, 2 + i + offset)) for offset in range(3)]
        couple(weights[i], present, moved_of(moved, (1,), i)[1], None, True)

    both = jnp.concatenate(
        [
            jnp.concatenate([pair[1], pair[2]], axis=1),
            jnp.concatenate([pair[5], pair[6]], axis=1),
        ],
        axis=0,
    )
    split = halves(both)
    forms = [split_product(halves(moved[u]), split, 1) for u in range(2)]
    tables = [forms[0][:, :W], forms[0][:, W:] + forms[1][:, :W], forms[1][:, W:]]
    square = product_t(both, both[W:])
    grams = [start_gram[...], square[:W] + square[:W].T, square[W:]]
    row, lane = iotas((HALF, W))

    def put(index, value):
        for y in range(8):
            blocks[pl.ds(24 * y + index, 8, stride=192), :] = value[8 * y : 8 * y + 8]

    for version in range(3):
        gram = grams[version]
        upper, under = gram[:HALF], gram[HALF:]
        for part in range(6):
            put(8 * version + part, tables[version][part * HALF : (part + 1) * HALF])
        fold = jnp.where(lane <= row + HALF, under, pltpu.roll(upper, HALF, 1))
        put(8 * version + 6, fold)
        diagonal = jnp.sum(jnp.where(lane == row, upper, 0.0), axis=1, keepdims=True)
        extra = jnp.where(lane == 0, diagonal, 0.0)
        if version == 0:
            extra = jnp.where(lane == 1, along, jnp.where(lane == 2, energy, extra))
        put(8 * version + 7, extra)


def local_part(mine, low, high, ahead, behind, terms, table, early, left_interface, right_interface):
    vmem = pl.BlockSpec(memory_space=pltpu.VMEM)
    return pl.pallas_call(
        local_kernel,
        out_shape=(
            pltpu.VMEM((HALF * 24, W), jnp.float32),
            pltpu.VMEM((2 * W, W), jnp.float32),
        ),
        in_specs=[vmem] * 11,
        out_specs=(vmem, vmem),
        scratch_shapes=[
            pltpu.VMEM((4, 3 * W, W), jnp.float32),
            pltpu.VMEM((6, W, 3 * W), jnp.float32),
            pltpu.VMEM((4, W, 3 * W), jnp.float32),
            pltpu.VMEM((2, 3 * W, 2 * W), jnp.float32),
            pltpu.VMEM((8, W, W), jnp.float32),
        ],
        compiler_params=pltpu.CompilerParams(vmem_limit_bytes=ROOM),
        name="local_part",
    )(
        *near(
            mine,
            low,
            high,
            ahead,
            behind,
            terms,
            table,
            *early,
            left_interface,
            right_interface,
        )
    )


def combine_kernel(got, out, alpha_ref, *, scale):
    count = got.shape[0] // 4
    parts = [jnp.sum(got[pl.ds(v, count, stride=4), :], axis=0, keepdims=True) for v in range(4)]
    lane = lax.broadcasted_iota(jnp.int32, (1, W), 1)
    along = jnp.sum(jnp.where(lane == 1, parts[3], 0.0), axis=1, keepdims=True)
    energy = jnp.sum(jnp.where(lane == 2, parts[3], 0.0), axis=1, keepdims=True)
    alpha = jnp.broadcast_to(along, (1, W)) / jnp.broadcast_to(energy, (1, W))
    alpha_ref[...] = jnp.broadcast_to(alpha, (8, W))
    block = (parts[0] + alpha * (parts[1] + alpha * parts[2])) * scale
    out[...] = jnp.broadcast_to(block, out.shape)


def combine_part(got, scale):
    vmem = pl.BlockSpec(memory_space=pltpu.VMEM)

    def kernel(*refs):
        combine_kernel(*refs, scale=scale)

    return pl.pallas_call(
        kernel,
        out_shape=(
            pltpu.VMEM((8, W), jnp.float32),
            pltpu.VMEM((8, W), jnp.float32),
        ),
        in_specs=[vmem],
        out_specs=(vmem, vmem),
        compiler_params=pltpu.CompilerParams(vmem_limit_bytes=ROOM),
        name="combine_part",
    )(*near(got))


def factor_kernel(whole, alpha_ref, mine, owned, basis, triangle, inverse, table):
    row, lane = iotas((HALF, W))
    fold = part_of(whole, 6)
    extra = part_of(whole, 7)
    under = jnp.where(lane <= row + HALF, fold, 0.0)
    upper = jnp.where((lane > row) & (lane < HALF), pltpu.roll(fold, HALF, 1), 0.0)
    upper = upper + jnp.where(lane == row, jnp.broadcast_to(extra[:, :1], (HALF, W)), 0.0)
    zero = jnp.zeros((HALF, W), jnp.float32)
    lower_part = jnp.concatenate([zero, under], axis=0)
    upper_part = jnp.concatenate([upper, zero], axis=0)
    row, lane = iotas((W, W))
    lower_part = lower_part + jnp.where(lane < row, upper_part.T, 0.0)
    table[:, :W] = lower_part.T + jnp.where(lane < row, lower_part, 0.0) + upper_part - jnp.where(
        lane > row, upper_part, 0.0
    )
    table[:, W:] = jnp.where(lane == row, 1.0, 0.0)

    sub, across = iotas((SIZE, W))
    for first in range(0, W, SIZE):
        last = first + SIZE
        panel = table[first:last, :]
        left, right = panel[:, :W], panel[:, W:]
        columns = [
            jnp.broadcast_to(left[:, first + k : first + k + 1], (SIZE, W)) for k in range(SIZE)
        ]
        for k in range(SIZE):
            pivot = jnp.broadcast_to(columns[k][k : k + 1, :], (SIZE, W))
            root = lax.rsqrt(pivot)
            root = root * (1.5 - 0.5 * pivot * (root * root))
            factor = jnp.where(sub > k, columns[k] * (root * root), 0.0)

            def spread(value):
                return jnp.broadcast_to(value[k : k + 1, :], (SIZE, W))

            for j in range(k + 1, SIZE):
                columns[j] = columns[j] - factor * spread(columns[j])
            head = spread(left)
            left = jnp.where(sub == k, head * root, left - factor * head)
            head = spread(right)
            right = jnp.where(sub == k, head * root, right - factor * head)
        left = jnp.where(across >= sub + first, left, 0.0)
        triangle[first:last, :] = left
        inverse[first:last, :] = right
        if last < W:
            done = jnp.concatenate([left, right], axis=1)
            turned = left.T
            for low, high in ((last, last + SIZE), (last + SIZE, W)):
                if low < high:
                    table[low:high, :] = table[low:high, :] - product(turned[low:high], done)

    alpha = alpha_ref[0:1, :]
    core = [
        mine[:, i].reshape(W, W) + alpha * owned[i * W : (i + 1) * W] for i in range(2)
    ]
    both = product(inverse[...], jnp.concatenate(core, axis=1))
    for i in range(2):
        basis[:, i] = both[:, i * W : (i + 1) * W].reshape(basis.shape[0], basis.shape[2], W)


def interface_kernel(rank, whole, inverse, out):
    rows = out.shape[1]
    start = pl.multiple_of(rank[0] * rows, rows)
    mine = inverse[pl.ds(start, rows), :]
    parts = []
    for beta in range(3):
        both = jnp.concatenate([part_of(whole, 2 * beta + h) for h in range(2)])
        parts.append(product(mine, both))
    result = product_t(jnp.concatenate(parts, axis=0), inverse[...])
    out[...] = result.reshape(3, rows, W)


def final_part(whole, alpha, mine, owned, rank):
    vmem = pl.BlockSpec(memory_space=pltpu.VMEM)
    ranks, _, piece, _ = mine.shape
    basis, triangle, inverse = pl.pallas_call(
        factor_kernel,
        out_shape=(
            pltpu.VMEM((ranks, 2, piece, W), jnp.float32),
            jax.ShapeDtypeStruct((W, W), jnp.float32),
            pltpu.VMEM((W, W), jnp.float32),
        ),
        in_specs=[vmem] * 4,
        out_specs=(vmem,) * 3,
        scratch_shapes=[pltpu.VMEM((W, 2 * W), jnp.float32)],
        compiler_params=pltpu.CompilerParams(vmem_limit_bytes=ROOM),
        name="factor_part",
    )(*near(whole, alpha, mine, owned))
    interface = pl.pallas_call(
        interface_kernel,
        out_shape=jax.ShapeDtypeStruct((3, piece, W), jnp.float32),
        in_specs=[pl.BlockSpec(memory_space=pltpu.SMEM), vmem, vmem],
        out_specs=vmem,
        compiler_params=pltpu.CompilerParams(vmem_limit_bytes=ROOM),
        name="interface_part",
    )(rank, *near(whole, inverse))
    return basis, triangle, interface


def shards(start_core, right_side, left_interface, right_interface, couplings):
    height, piece, width = start_core.shape
    ranks = lax.axis_size("rank")
    slabs = lax.axis_size(("x", "y", "core"))
    count = slabs * ranks
    own = height // ranks
    assert width == W and own == 2 and slabs == HALF
    rank_index = lax.axis_index("rank")
    scale = 1.0 / (height * slabs * width)

    start = start_core.reshape(ranks, own, piece, width)
    right = right_side.reshape(ranks, own, piece, width)
    odd = lax.axis_index("core") == 1
    packed = jnp.concatenate([start, right], axis=1)
    mine = exchange(jnp.where(odd, packed[::-1], packed), "rank")

    chunk = jnp.where(odd, ranks - 1 - rank_index, rank_index)
    table = lax.dynamic_slice_in_dim(couplings.reshape(27, height), chunk * own, own, 1)
    table = jnp.pad(table, ((0, 5), (0, 0))).T[:, :, None]
    table = jnp.broadcast_to(table, (own, 32, width)).reshape(own * 32, width)
    order = [
        slab * ranks + (part if slab % 2 == 0 else ranks - 1 - part)
        for slab in range(slabs)
        for part in range(ranks)
    ]
    forward = list(zip(order[:-1], order[1:]))
    backward = [(target, source) for source, target in forward]

    ahead, behind, terms = parcel_part(mine, table, left_interface, right_interface)
    low = lax.ppermute(ahead, ("x", "y", "core", "rank"), forward)
    high = lax.ppermute(behind, ("x", "y", "core", "rank"), backward)
    early = early_part(mine, table, left_interface)
    blocks, owned = local_part(
        mine, low, high, ahead, behind, terms, table, early, left_interface, right_interface
    )

    block = jnp.sum(exchange(blocks.reshape(8, 192, width), ("x", "core")), axis=0)
    block = block.reshape(8, 3, 8, width)
    sums = jnp.broadcast_to(block[:1, :1, 7:, :], (8, 8, 1, width))
    block = jnp.concatenate([block.transpose(0, 2, 1, 3), sums], axis=2)
    block = exchange(block.reshape(64, 4, width), ("y", "rank")).reshape(256, width)
    block, alpha = combine_part(block, scale)
    block = exchange(block.reshape(8, 1, width), ("x", "core")).reshape(8, width)
    whole = exchange(jnp.broadcast_to(block, (64, 8, width)), ("y", "rank"))

    rank = jnp.full((1,), rank_index, jnp.int32)
    basis, triangle, interface = final_part(whole.reshape(512, width), alpha, mine, owned, rank)
    output = exchange(basis, "rank")
    output = jnp.where(odd, output[::-1], output).reshape(height, piece, width)
    return (output, triangle, interface)


def solution(mesh):
    names = ("x", "y", "core")
    fine = Mesh(mesh.devices.reshape(4, 8, 2, 8), names + ("rank",))
    placed = (P(names, "rank", None), P(names, "rank", None), P(), P(), P(None, None, None, names))
    return jax.shard_map(
        shards,
        mesh=fine,
        in_specs=placed,
        out_specs=(P(names, "rank", None), P(), P(None, "rank", None)),
        check_vma=False,
    )
```

```python
import jax
import jax.numpy as jnp
from jax import lax
from jax.experimental import pallas as pl
from jax.experimental.pallas import tpu as pltpu
from jax.sharding import Mesh
from jax.sharding import PartitionSpec as P

highest = lax.Precision.HIGHEST
W = 128
HALF = W // 2
SIZE = 8
ROOM = 16 * 2**20


def exchange(blocks, axis):
    return lax.all_to_all(blocks, axis, 0, 0, tiled=True)


def product(left, right):
    return jnp.dot(left, right, precision=highest, preferred_element_type=jnp.float32)


def product_t(left, right):
    return lax.dot_general(
        left,
        right,
        (((1,), (1,)), ((), ())),
        precision=highest,
        preferred_element_type=jnp.float32,
    )


def halves(value):
    high = value.astype(jnp.bfloat16)
    return high, (value - high.astype(jnp.float32)).astype(jnp.bfloat16)


def split_product(left, right, contract):
    def one(a, b):
        return lax.dot_general(
            a, b, (((1,), (contract,)), ((), ())), preferred_element_type=jnp.float32
        )

    return one(left[0], right[0]) + (one(left[0], right[1]) + one(left[1], right[0]))


def iotas(shape):
    return lax.broadcasted_iota(jnp.int32, shape, 0), lax.broadcasted_iota(jnp.int32, shape, 1)


def near(*values):
    return [pltpu.with_memory_space_constraint(value, pltpu.VMEM) for value in values]


def own_slot(mine, index):
    return mine[:, index].reshape(W, W)


def contract(right_rows, values, terms, first):
    for k in range(0, len(values), 2):
        both = split_product(right_rows, halves(jnp.concatenate(values[k : k + 2], axis=1)), 0)
        terms[first + k] = both[:, :W]
        terms[first + k + 1] = both[:, W:]


def couple(place, sources, target, base, left_first):
    used = {offset for offset, _ in sources}
    weight = {
        (i, j, offset): jnp.broadcast_to(place(i, j, offset), (8, W))
        for i in range(3)
        for j in range(3)
        for offset in used
    }

    def step(chunk, carry):
        at = pl.multiple_of(chunk * 8, 8)
        sums = [None if base is None else base(index, at) for index in range(3)]
        for offset, rows in sources:
            for inner in range(3):
                value = rows(inner, at)
                for outer in range(3):
                    key = (inner, outer) if left_first else (outer, inner)
                    part = weight[key + (offset,)] * value
                    sums[outer] = part if sums[outer] is None else sums[outer] + part
        for index in range(3):
            target(index, at, sums[index])
        return carry

    lax.fori_loop(0, W // 8, step, 0, unroll=2)


def term_rows(terms, place):
    return lambda index, at: terms[place, pl.ds(index * W + at, 8), :]


def mixed_rows(mixed, place):
    return lambda index, at: mixed[place, pl.ds(at, 8), index * W : (index + 1) * W]


def lanes_of(ref, place):
    def load(index, at):
        return ref[place, pl.ds(at, 8), index * W : (index + 1) * W]

    def store(index, at, value):
        ref[place, pl.ds(at, 8), index * W : (index + 1) * W] = value

    return load, store


def moved_of(ref, lead, place):
    def load(index, at):
        return ref[lead + (pl.ds(index * W + at, 8), slice(place * W, (place + 1) * W))]

    def store(index, at, value):
        ref[lead + (pl.ds(index * W + at, 8), slice(place * W, (place + 1) * W))] = value

    return load, store


def own_row(table, mode):
    def row(i, j, offset):
        at = 32 * mode + 9 * i + 3 * j + offset
        return table[at : at + 1, :]

    return row


def sent_row(parcel):
    return lambda i, j, offset: parcel[2 * W + 3 * i + j : 2 * W + 3 * i + j + 1, :]


def parcel_kernel(mine, table, left_ref, right_ref, ahead, behind, terms, coupled):
    right_rows = halves(right_ref[...].reshape(3 * W, W))
    left_lanes = halves(jnp.concatenate([left_ref[0], left_ref[1], left_ref[2]], axis=1))
    contract(right_rows, [own_slot(mine, 0), own_slot(mine, 1)], terms, 0)
    for i in range(2):
        present = [(1 - i + k, term_rows(terms, k)) for k in range(2)]
        couple(own_row(table, i), present, lanes_of(coupled, i)[1], None, False)
    applied = split_product(halves(coupled[...].reshape(2 * W, 3 * W)), left_lanes, 1)
    for i, parcel, offset in ((0, behind, 0), (1, ahead, 2)):
        parcel[0:W] = own_slot(mine, i)
        parcel[W : 2 * W] = own_slot(mine, 2 + i) - applied[i * W : (i + 1) * W]
        parcel[2 * W : 2 * W + 16] = jnp.zeros((16, W), jnp.float32)
        row = own_row(table, i)
        for alpha in range(3):
            for beta in range(3):
                at = 2 * W + 3 * alpha + beta
                parcel[at : at + 1, :] = row(alpha, beta, offset)


def parcel_part(mine, table, left_interface, right_interface):
    vmem = pl.BlockSpec(memory_space=pltpu.VMEM)
    return pl.pallas_call(
        parcel_kernel,
        out_shape=(
            pltpu.VMEM((2 * W + 16, W), jnp.float32),
            pltpu.VMEM((2 * W + 16, W), jnp.float32),
            pltpu.VMEM((2, 3 * W, W), jnp.float32),
        ),
        in_specs=[vmem] * 4,
        out_specs=(vmem,) * 3,
        scratch_shapes=[pltpu.VMEM((2, W, 3 * W), jnp.float32)],
        compiler_params=pltpu.CompilerParams(vmem_limit_bytes=ROOM),
        name="parcel_part",
    )(*near(mine, table, left_interface, right_interface))


def early_kernel(mine, table, left_ref, shifted, mixed):
    left_rows = halves(left_ref[...].reshape(3 * W, W))
    stack = halves(jnp.concatenate([own_slot(mine, 0), own_slot(mine, 1)], axis=0))
    mixed[...] = split_product(stack, left_rows, 1).reshape(2, W, 3 * W)
    for i in range(2):
        present = [(1 - i + k, mixed_rows(mixed, k)) for k in range(2)]
        couple(own_row(table, i), present, moved_of(shifted, (), i)[1], None, True)


def early_part(mine, table, left_interface):
    vmem = pl.BlockSpec(memory_space=pltpu.VMEM)
    return pl.pallas_call(
        early_kernel,
        out_shape=pltpu.VMEM((3 * W, 2 * W), jnp.float32),
        in_specs=[vmem] * 3,
        out_specs=vmem,
        scratch_shapes=[pltpu.VMEM((2, W, 3 * W), jnp.float32)],
        compiler_params=pltpu.CompilerParams(vmem_limit_bytes=ROOM),
        name="early_part",
    )(*near(mine, table, left_interface))


def local_kernel(
    mine,
    low,
    high,
    ahead,
    behind,
    own_terms,
    table,
    shifted,
    left_ref,
    right_ref,
    blocks,
    owned,
    terms,
    mixed,
    coupled,
    moved,
    pair,
):
    weights = [own_row(table, 0), own_row(table, 1)]
    right_rows = halves(right_ref[...].reshape(3 * W, W))
    left_rows = halves(left_ref[...].reshape(3 * W, W))
    left_lanes = halves(jnp.concatenate([left_ref[0], left_ref[1], left_ref[2]], axis=1))
    contract(right_rows, [low[0:W], high[0:W]], terms, 0)
    places = [
        (sent_row(low), (2, term_rows(own_terms, 0))),
        (weights[0], (0, term_rows(terms, 0))),
        (weights[1], (2, term_rows(terms, 1))),
        (sent_row(high), (0, term_rows(own_terms, 1))),
    ]
    for i in range(4):
        couple(places[i][0], [places[i][1]], lanes_of(coupled, i)[1], None, False)
    applied = split_product(halves(coupled[...].reshape(4 * W, 3 * W)), left_lanes, 1)
    residual = [
        source[W : 2 * W] - applied[i * W : (i + 1) * W]
        for i, source in enumerate((low, behind, ahead, high))
    ]
    outer = [None, low[0:W], high[0:W]]
    pair[0], pair[3] = outer[1], outer[2]
    pair[1], pair[2] = own_slot(mine, 0), own_slot(mine, 1)
    for i in range(4):
        pair[4 + i] = residual[i]
    owned[0:W] = residual[1]
    owned[W : 2 * W] = residual[2]
    contract(right_rows, residual, terms, 0)
    along = jnp.zeros((1, 1), jnp.float32)
    energy = jnp.zeros((1, 1), jnp.float32)
    for i in range(2):
        present = [(offset, term_rows(terms, i + offset)) for offset in range(3)]
        couple(weights[i], present, lanes_of(coupled, i)[1], None, False)
    images = split_product(halves(coupled[0:2].reshape(2 * W, 3 * W)), left_lanes, 1)
    for i in range(2):
        image = images[i * W : (i + 1) * W]
        along = along + jnp.sum(pair[5 + i] * image, keepdims=True)
        energy = energy + jnp.sum(image * image, keepdims=True)

    stack = halves(jnp.concatenate([outer[1], outer[2]] + residual, axis=0))
    mixed[...] = split_product(stack, left_rows, 1).reshape(6, W, 3 * W)
    for i in range(2):
        base = moved_of(shifted, (), i)[0]
        present = [(2 * i, mixed_rows(mixed, i))]
        couple(weights[i], present, moved_of(moved, (0,), i)[1], base, True)
        present = [(offset, mixed_rows(mixed, 2 + i + offset)) for offset in range(3)]
        couple(weights[i], present, moved_of(moved, (1,), i)[1], None, True)

    both = jnp.concatenate(
        [
            jnp.concatenate([pair[1], pair[2]], axis=1),
            jnp.concatenate([pair[5], pair[6]], axis=1),
        ],
        axis=0,
    )
    split = halves(both)
    forms = [split_product(halves(moved[u]), split, 1) for u in range(2)]
    tables = [forms[0][:, :W], forms[0][:, W:] + forms[1][:, :W], forms[1][:, W:]]
    square = product_t(both, both)
    grams = [square[:W, :W], square[:W, W:] + square[W:, :W], square[W:, W:]]
    row, lane = iotas((HALF, W))
    for version in range(3):
        gram = grams[version]
        upper, under = gram[:HALF], gram[HALF:]
        for part in range(6):
            blocks[pl.ds(8 * version + part, HALF, stride=24), :] = tables[version][
                part * HALF : (part + 1) * HALF
            ]
        fold = jnp.where(lane <= row + HALF, under, pltpu.roll(upper, HALF, 1))
        blocks[pl.ds(8 * version + 6, HALF, stride=24), :] = fold
        diagonal = jnp.sum(jnp.where(lane == row, upper, 0.0), axis=1, keepdims=True)
        extra = jnp.where(lane == 0, diagonal, 0.0)
        if version == 0:
            extra = jnp.where(lane == 1, along, jnp.where(lane == 2, energy, extra))
        blocks[pl.ds(8 * version + 7, HALF, stride=24), :] = extra


def local_part(mine, low, high, ahead, behind, terms, table, shifted, left_interface, right_interface):
    vmem = pl.BlockSpec(memory_space=pltpu.VMEM)
    return pl.pallas_call(
        local_kernel,
        out_shape=(
            pltpu.VMEM((HALF * 24, W), jnp.float32),
            pltpu.VMEM((2 * W, W), jnp.float32),
        ),
        in_specs=[vmem] * 10,
        out_specs=(vmem, vmem),
        scratch_shapes=[
            pltpu.VMEM((4, 3 * W, W), jnp.float32),
            pltpu.VMEM((6, W, 3 * W), jnp.float32),
            pltpu.VMEM((4, W, 3 * W), jnp.float32),
            pltpu.VMEM((2, 3 * W, 2 * W), jnp.float32),
            pltpu.VMEM((8, W, W), jnp.float32),
        ],
        compiler_params=pltpu.CompilerParams(vmem_limit_bytes=ROOM),
        name="local_part",
    )(
        *near(
            mine,
            low,
            high,
            ahead,
            behind,
            terms,
            table,
            shifted,
            left_interface,
            right_interface,
        )
    )


def combine_kernel(got, out, alpha_ref, *, scale):
    count = got.shape[0] // 4
    parts = [jnp.sum(got[pl.ds(v, count, stride=4), :], axis=0, keepdims=True) for v in range(4)]
    lane = lax.broadcasted_iota(jnp.int32, (1, W), 1)
    along = jnp.sum(jnp.where(lane == 1, parts[3], 0.0), axis=1, keepdims=True)
    energy = jnp.sum(jnp.where(lane == 2, parts[3], 0.0), axis=1, keepdims=True)
    alpha = jnp.broadcast_to(along, (1, W)) / jnp.broadcast_to(energy, (1, W))
    alpha_ref[...] = jnp.broadcast_to(alpha, (8, W))
    block = (parts[0] + alpha * (parts[1] + alpha * parts[2])) * scale
    out[...] = jnp.broadcast_to(block, out.shape)


def combine_part(got, scale):
    vmem = pl.BlockSpec(memory_space=pltpu.VMEM)

    def kernel(*refs):
        combine_kernel(*refs, scale=scale)

    return pl.pallas_call(
        kernel,
        out_shape=(
            pltpu.VMEM((got.shape[0] // 4, W), jnp.float32),
            pltpu.VMEM((8, W), jnp.float32),
        ),
        in_specs=[vmem],
        out_specs=(vmem, vmem),
        compiler_params=pltpu.CompilerParams(vmem_limit_bytes=ROOM),
        name="combine_part",
    )(*near(got))


def factor_kernel(whole, alpha_ref, mine, owned, basis, triangle, inverse, table):
    row, lane = iotas((HALF, W))
    fold = whole[pl.ds(6, HALF, stride=8), :]
    extra = whole[pl.ds(7, HALF, stride=8), :]
    under = jnp.where(lane <= row + HALF, fold, 0.0)
    upper = jnp.where((lane > row) & (lane < HALF), pltpu.roll(fold, HALF, 1), 0.0)
    upper = upper + jnp.where(lane == row, jnp.broadcast_to(extra[:, :1], (HALF, W)), 0.0)
    zero = jnp.zeros((HALF, W), jnp.float32)
    lower_part = jnp.concatenate([zero, under], axis=0)
    upper_part = jnp.concatenate([upper, zero], axis=0)
    row, lane = iotas((W, W))
    lower_part = lower_part + jnp.where(lane < row, upper_part.T, 0.0)
    table[:, :W] = lower_part.T + jnp.where(lane < row, lower_part, 0.0) + upper_part - jnp.where(
        lane > row, upper_part, 0.0
    )
    table[:, W:] = jnp.where(lane == row, 1.0, 0.0)

    sub, across = iotas((SIZE, W))
    for first in range(0, W, SIZE):
        last = first + SIZE
        panel = table[first:last, :]
        left, right = panel[:, :W], panel[:, W:]
        columns = [
            jnp.broadcast_to(left[:, first + k : first + k + 1], (SIZE, W)) for k in range(SIZE)
        ]
        for k in range(SIZE):
            pivot = jnp.broadcast_to(columns[k][k : k + 1, :], (SIZE, W))
            root = lax.rsqrt(pivot)
            root = root * (1.5 - 0.5 * pivot * (root * root))
            factor = jnp.where(sub > k, columns[k] * (root * root), 0.0)

            def spread(value):
                return jnp.broadcast_to(value[k : k + 1, :], (SIZE, W))

            for j in range(k + 1, SIZE):
                columns[j] = columns[j] - factor * spread(columns[j])
            head = spread(left)
            left = jnp.where(sub == k, head * root, left - factor * head)
            head = spread(right)
            right = jnp.where(sub == k, head * root, right - factor * head)
        left = jnp.where(across >= sub + first, left, 0.0)
        triangle[first:last, :] = left
        inverse[first:last, :] = right
        if last < W:
            done = jnp.concatenate([left, right], axis=1)
            turned = left.T
            for low, high in ((last, last + SIZE), (last + SIZE, W)):
                if low < high:
                    table[low:high, :] = table[low:high, :] - product(turned[low:high], done)

    alpha = alpha_ref[0:1, :]
    core = [
        mine[:, i].reshape(W, W) + alpha * owned[i * W : (i + 1) * W] for i in range(2)
    ]
    both = product(inverse[...], jnp.concatenate(core, axis=1))
    for i in range(2):
        basis[:, i] = both[:, i * W : (i + 1) * W].reshape(basis.shape[0], basis.shape[2], W)


def interface_kernel(rank, whole, inverse, out):
    rows = out.shape[1]
    start = pl.multiple_of(rank[0] * rows, rows)
    mine = inverse[pl.ds(start, rows), :]
    parts = []
    for beta in range(3):
        halves = [whole[pl.ds(2 * beta + h, HALF, stride=8), :] for h in range(2)]
        parts.append(product(mine, jnp.concatenate(halves, axis=0)))
    result = product_t(jnp.concatenate(parts, axis=0), inverse[...])
    out[...] = result.reshape(3, rows, W)


def final_part(whole, alpha, mine, owned, rank):
    vmem = pl.BlockSpec(memory_space=pltpu.VMEM)
    ranks, _, piece, _ = mine.shape
    basis, triangle, inverse = pl.pallas_call(
        factor_kernel,
        out_shape=(
            pltpu.VMEM((ranks, 2, piece, W), jnp.float32),
            jax.ShapeDtypeStruct((W, W), jnp.float32),
            pltpu.VMEM((W, W), jnp.float32),
        ),
        in_specs=[vmem] * 4,
        out_specs=(vmem,) * 3,
        scratch_shapes=[pltpu.VMEM((W, 2 * W), jnp.float32)],
        compiler_params=pltpu.CompilerParams(vmem_limit_bytes=ROOM),
        name="factor_part",
    )(*near(whole, alpha, mine, owned))
    interface = pl.pallas_call(
        interface_kernel,
        out_shape=jax.ShapeDtypeStruct((3, piece, W), jnp.float32),
        in_specs=[pl.BlockSpec(memory_space=pltpu.SMEM), vmem, vmem],
        out_specs=vmem,
        compiler_params=pltpu.CompilerParams(vmem_limit_bytes=ROOM),
        name="interface_part",
    )(rank, *near(whole, inverse))
    return basis, triangle, interface


def shards(start_core, right_side, left_interface, right_interface, couplings):
    height, piece, width = start_core.shape
    ranks = lax.axis_size("rank")
    slabs = lax.axis_size(("x", "y", "core"))
    count = slabs * ranks
    own = height // ranks
    assert width == W and own == 2 and slabs == HALF
    rank_index = lax.axis_index("rank")
    scale = 1.0 / (height * slabs * width)

    start = start_core.reshape(ranks, own, piece, width)
    right = right_side.reshape(ranks, own, piece, width)
    odd = lax.axis_index("core") == 1
    packed = jnp.concatenate([start, right], axis=1)
    mine = exchange(jnp.where(odd, packed[::-1], packed), "rank")

    chunk = jnp.where(odd, ranks - 1 - rank_index, rank_index)
    table = lax.dynamic_slice_in_dim(couplings.reshape(27, height), chunk * own, own, 1)
    table = jnp.pad(table, ((0, 5), (0, 0))).T[:, :, None]
    table = jnp.broadcast_to(table, (own, 32, width)).reshape(own * 32, width)
    order = [
        slab * ranks + (part if slab % 2 == 0 else ranks - 1 - part)
        for slab in range(slabs)
        for part in range(ranks)
    ]
    forward = list(zip(order[:-1], order[1:]))
    backward = [(target, source) for source, target in forward]

    ahead, behind, terms = parcel_part(mine, table, left_interface, right_interface)
    low = lax.ppermute(ahead, ("x", "y", "core", "rank"), forward)
    high = lax.ppermute(behind, ("x", "y", "core", "rank"), backward)
    shifted = early_part(mine, table, left_interface)
    blocks, owned = local_part(
        mine, low, high, ahead, behind, terms, table, shifted, left_interface, right_interface
    )

    block = jnp.sum(exchange(blocks.reshape(8, 192, width), ("x", "core")), axis=0)
    block = block.reshape(8, 3, 8, width)
    sums = jnp.broadcast_to(block[:1, :1, 7:, :], (8, 8, 1, width))
    block = jnp.concatenate([block.transpose(0, 2, 1, 3), sums], axis=2)
    block = exchange(block.reshape(64, 4, width), ("y", "rank")).reshape(256, width)
    block, alpha = combine_part(block, scale)
    block = exchange(block.reshape(64, 1, width), ("y", "rank")).reshape(64, width)
    whole = exchange(jnp.broadcast_to(block, (8, 64, width)), ("x", "core"))

    rank = jnp.full((1,), rank_index, jnp.int32)
    basis, triangle, interface = final_part(whole.reshape(512, width), alpha, mine, owned, rank)
    output = exchange(basis, "rank")
    output = jnp.where(odd, output[::-1], output).reshape(height, piece, width)
    return (output, triangle, interface)


def solution(mesh):
    names = ("x", "y", "core")
    fine = Mesh(mesh.devices.reshape(4, 8, 2, 8), names + ("rank",))
    placed = (P(names, "rank", None), P(names, "rank", None), P(), P(), P(None, None, None, names))
    return jax.shard_map(
        shards,
        mesh=fine,
        in_specs=placed,
        out_specs=(P(names, "rank", None), P(), P(None, "rank", None)),
        check_vma=False,
    )
```
